32 devices in a mesh: slab: 8 (over z, x), pen: 4 (over y, core).
Axes of the slice: x: 2, y: 2, z: 4, core: 2. Of those that a mesh axis runs over, the one named last changes fastest.
Arguments:
- charges: bfloat16 [1024, 128], P(('slab', 'pen')), may hold values from -6 to 6
- counts: int32 [1024], P(('slab', 'pen')), may hold values from 32 to 128
- proj_weight: bfloat16 [1024, 128, 128], P(('slab', 'pen')), may hold values from -0.5 to 0.5
- dest_slab: int32 [1024, 1], P(('slab', 'pen')), may hold values from 0 to 3; in each aligned block of 32 rows (0 to 31, 32 to 63, ...) at most 16 rows name the same one
- box_index: int32 [1024], P(('slab', 'pen')), may hold values from 0 to 8191
- pair_target: int32 [2048], P(('slab', 'pen')), may hold values from 0 to 31
- pair_source: int32 [2048], P(('slab', 'pen')), may hold values from 0 to 31
- near_matrix: bfloat16 [2048, 128, 128], P(('slab', 'pen')), may hold values from -0.5 to 0.5
- kernel_hat: float32 [2, 256, 256, 512], P(None, None, 'slab', 'pen'), may hold values from -8 to 8, as said below
Outputs:
- potential: bfloat16 [1024, 128], P(('slab', 'pen'))
The draws below stay inside these ranges and needn't reach their ends.
Inputs may be any that keep to these rules, and one draw needn't show every extreme that they name: `dest_slab`: each block's box lies in the lower half of the depth; among the 32 blocks of one device no slab is named more than 16 times. `pair_target`: local indices of blocks held by the same device as the pair. `pair_source`: local indices of blocks held by the same device as the pair. Hermitian, as the transform of a real kernel: with indices taken modulo 256, 256 and 512, kernel_hat[0] at (-u, -v, -w) equals kernel_hat[0] at (u, v, w), and kernel_hat[1] at (-u, -v, -w) equals minus kernel_hat[1] at (u, v, w).
All inputs are finite; a program needn't handle non-finite values.
Results may differ from the reference program's by a relative error of at most 0.0039.
Values may be sent and summed in bfloat16 or wider, within the bound.
No kernel may reach another device: no remote copies, remote signals or barrier semaphores. Data moves between devices by JAX's collectives and lax.ppermute only.
A program may use at most 128 MiB of HBM per device.

```python
import math
import jax
import jax.numpy as jnp
import numpy as np
from jax import lax

X = 512
Y = 256
Z = 256
PB = 128
STENCIL = 128
BLK_DEV = 32
PAIRS_DEV = 64
CAP = 16
BLOCKS = 1024
PAIRS = 2048
N_SLAB = 8
N_PEN = 4
DEVICES = 32


def mirrored(field):
    for axis_id in range(3):
        field = jnp.roll(jnp.flip(field, axis_id), 1, axis_id)
    return field


def draw_kernel_hat(key, part):
    first_key = jax.random.fold_in(key, 11)
    second_key = jax.random.fold_in(key, 23)
    even_base = jnp.clip(0.7 * jax.random.normal(first_key, (Z, Y, X), jnp.float32), -4.0, 4.0)
    odd_base = jnp.clip(0.7 * jax.random.normal(second_key, (Z, Y, X), jnp.float32), -4.0, 4.0)
    real_part = even_base + mirrored(even_base)
    imag_part = odd_base - mirrored(odd_base)
    return jnp.stack([real_part, imag_part]).astype(jnp.float32)


def with_ends(values, stream_key, smallest, largest):
    longest = values.shape.index(max(values.shape))
    spots = []
    for shift in (0, 1):
        where = [jax.random.randint(jax.random.fold_in(stream_key, axis), (), 0, length) for axis, length in enumerate(values.shape)]
        where[longest] = (where[longest] + shift) % values.shape[longest]
        spots.append(tuple(where))
    return values.at[spots[0]].set(smallest).at[spots[1]].set(largest)


def steps_of(key, extent, cuts, least, high):
    factor_of, own = 1.0, jax.random.fold_in(key, 6)
    for position, parts in cuts:
        heights = jnp.exp(jax.random.uniform(jax.random.fold_in(own, position), (parts,), jnp.float32, least / len(cuts), high / len(cuts)))
        factor_of = factor_of * jnp.repeat(heights, extent[position] // parts).reshape([-1 if axis == position else 1 for axis in range(len(extent))])
    return factor_of


def deal_out(rng, own, number, rows, count, top, reach, lean):
    order = jax.random.permutation(rng, count)
    heavy_load, usual = load_shares(count, rows * top, reach, lean, True), load_shares(count, rows * top, reach, lean, False)
    places = jnp.arange(count)

    def named(tallies, offset_by):
        used = int((tallies > 0).sum())
        fixed = max(1, used // 4)
        passed = fixed + (places - fixed + offset_by * (used - fixed)) % max(1, count - fixed)
        return jnp.zeros((count,), jnp.int32).at[order[jnp.where(places < fixed, places, passed)]].set(jnp.asarray(tallies, jnp.int32))

    tallies = jnp.where(number % 4 == 0, named(heavy_load, number // 4), named(usual, number - number // 4 - 1))
    mixed = jax.random.permutation(jax.random.fold_in(own, 3), count)
    giver, sink = mixed[0:count // 2 * 2:2], mixed[1:count // 2 * 2:2]
    slack = jnp.minimum(tallies[giver] - 1, reach - tallies[sink]) // 2
    slack = jnp.where((giver == order[0]) | (sink == order[0]) | (tallies[sink] == 0), 0, jnp.maximum(slack, 0))
    passed = jax.random.randint(jax.random.fold_in(own, 4), (count // 2,), 0, 1 << 20) % (slack + 1)
    tallies = tallies.at[giver].add(-passed).at[sink].add(passed)
    items = jnp.searchsorted(jnp.cumsum(tallies), jnp.arange(rows * top), side="right").astype(jnp.int32)
    table = items.reshape(top, rows).T
    table = table[jax.random.permutation(jax.random.fold_in(own, 1), rows)]
    offset_by = jax.random.randint(jax.random.fold_in(own, 2), (rows, 1), 0, top)
    return jnp.take_along_axis(table, (jnp.arange(top)[None, :] + offset_by) % top, axis=1)


def load_shares(number_of, total, reach, skew, full):
    loads = [(1 << 20) // math.isqrt(rank ** skew) + 1 for rank in range(1, number_of + 1)]
    largest = reach if full else min(reach, max(-(-total // number_of), total * loads[0] // sum(loads)))
    least = 1 if total - largest >= number_of - 1 else 0
    holding, surplus = [largest] + [least] * (number_of - 1), total - largest - least * (number_of - 1)
    while surplus > 0:
        movable = [i for i in range(1, number_of) if holding[i] < largest] or [i for i in range(1, number_of) if holding[i] < reach]
        pool, budget = sum([loads[i] for i in movable]), surplus
        for i in movable:
            addition = min(reach - holding[i], max(1, budget * loads[i] // pool), surplus)
            holding[i] = holding[i] + addition
            surplus = surplus - addition
    return np.array(holding)


def normal_values(key, shape, scale, bound, pieces=(), held_as=jnp.bfloat16):
    drawn = scale * jax.random.normal(key, shape, jnp.float32)
    if pieces:
        drawn = drawn * steps_of(key, shape, pieces, -0.22, 0.18)
    return jnp.clip(drawn, -bound, bound).astype(held_as)


def setup_inputs(seed: int = 0) -> dict:
    keys = jax.random.split(jax.random.key(seed), 10)
    charges = normal_values(keys[0], (BLOCKS, PB), 1.0, 6.0, ((0, 32),))
    counts = with_ends(jax.random.randint(keys[1], (BLOCKS,), PB // 4, PB + 1), jax.random.fold_in(keys[1], 1), PB // 4, PB).astype(jnp.int32)
    proj_weight = normal_values(keys[2], (BLOCKS, PB, STENCIL), STENCIL ** -0.5, 0.5, ((0, 32),))
    dest_slab_keys = jax.random.split(jax.random.fold_in(keys[3], 1), BLOCKS // BLK_DEV)
    dest_slab_turns = jax.random.permutation(jax.random.fold_in(keys[3], 3), BLOCKS // BLK_DEV)
    dest_slab = jax.vmap(lambda own, number: deal_out(jax.random.fold_in(keys[3], 2), own, number, BLK_DEV, N_SLAB // 2, 1, CAP, 2))(dest_slab_keys, dest_slab_turns).reshape((BLOCKS, 1))
    box_index = with_ends(jax.random.randint(keys[4], (BLOCKS,), 0, (Z // N_SLAB // 4) * (Y // N_PEN // 4) * (X // 8)), jax.random.fold_in(keys[4], 1), 0, ((Z // N_SLAB // 4) * (Y // N_PEN // 4) * (X // 8)) - 1).astype(jnp.int32)
    pair_target = with_ends(jax.random.randint(keys[5], (PAIRS,), 0, BLK_DEV), jax.random.fold_in(keys[5], 1), 0, BLK_DEV - 1).astype(jnp.int32)
    pair_source = with_ends(jax.random.randint(keys[6], (PAIRS,), 0, BLK_DEV), jax.random.fold_in(keys[6], 1), 0, BLK_DEV - 1).astype(jnp.int32)
    near_matrix = normal_values(keys[7], (PAIRS, PB, PB), PB ** -0.5, 0.5, ((0, 32),))
    kernel_hat = draw_kernel_hat(jax.random.fold_in(keys[9], 71), 0)
    return {"charges": charges, "counts": counts, "proj_weight": proj_weight, "dest_slab": dest_slab, "box_index": box_index, "pair_target": pair_target, "pair_source": pair_source, "near_matrix": near_matrix, "kernel_hat": kernel_hat}


def reference(charges, counts, proj_weight, dest_slab, box_index, pair_target, pair_source, near_matrix, kernel_hat):
    planes = Z // N_SLAB
    rows_pen = Y // N_PEN
    slot_ids = jnp.arange(PB, dtype=jnp.int32)
    live = slot_ids[None, :] < counts[:, None]
    charge = jnp.where(live, charges, jnp.zeros_like(charges))
    charge_dev = charge.reshape(DEVICES, BLK_DEV, PB)
    weight_dev = proj_weight.reshape(DEVICES, BLK_DEV, PB, STENCIL)

    def project(items):
        weights, block_charge = items
        return jnp.einsum('bp,bps->bs', block_charge.astype(jnp.float32), weights.astype(jnp.float32))
    spread = lax.map(project, (weight_dev, charge_dev)).reshape(BLOCKS, STENCIL)
    owner = jnp.arange(BLOCKS, dtype=jnp.int32) // BLK_DEV
    pen_index = owner % N_PEN
    per_row = X // 8
    per_plane = rows_pen // 4 * per_row
    box_z = box_index // per_plane
    box_y = box_index // per_row % (rows_pen // 4)
    box_x = box_index % per_row
    offsets = jnp.arange(STENCIL, dtype=jnp.int32)
    depth_cell = dest_slab[:, 0][:, None] * planes + 4 * box_z[:, None] + offsets[None, :] // 32
    row_cell = pen_index[:, None] * rows_pen + 4 * box_y[:, None] + offsets[None, :] // 8 % 4
    col_cell = 8 * box_x[:, None] + offsets[None, :] % 8
    flat = ((depth_cell * Y + row_cell) * X + col_cell).astype(jnp.int32)
    charge_grid = jnp.zeros((Z * Y * X,), jnp.float32).at[flat.reshape(-1)].add(spread.reshape(-1)).reshape(Z, Y, X)
    spectrum = jnp.fft.fftn(charge_grid)
    kernel = lax.complex(kernel_hat[0], kernel_hat[1])
    factor = math.sqrt(Z * Y * X / (BLOCKS * STENCIL))
    potential_grid = (jnp.real(jnp.fft.ifftn(kernel * spectrum)) * factor).astype(jnp.float32)
    samples = potential_grid.reshape(-1)[flat].astype(jnp.bfloat16)
    sample_dev = samples.reshape(DEVICES, BLK_DEV, STENCIL)

    def interpolate(items):
        weights, sampled = items
        return jnp.einsum('bps,bs->bp', weights.astype(jnp.float32), sampled.astype(jnp.float32))
    far = lax.map(interpolate, (weight_dev, sample_dev)).reshape(BLOCKS, PB)
    matrices = near_matrix.reshape(DEVICES, PAIRS_DEV, PB, PB)
    targets = pair_target.reshape(DEVICES, PAIRS_DEV)
    sources = pair_source.reshape(DEVICES, PAIRS_DEV)

    def correct(items):
        mats, target_ids, source_ids, block_charge = items
        driven = block_charge[source_ids].astype(jnp.float32)
        terms = jnp.einsum('tpq,tq->tp', mats.astype(jnp.float32), driven)
        return jnp.zeros((BLK_DEV, PB), jnp.float32).at[target_ids].add(terms)
    near = lax.map(correct, (matrices, targets, sources, charge_dev)).reshape(BLOCKS, PB)
    total = jnp.where(live, far + near, jnp.zeros_like(far))
    return total.astype(jnp.bfloat16)
```

```python
import functools
import math

import jax
import jax.numpy as jnp
import ml_dtypes
import numpy as np
from jax import lax
from jax.experimental import pallas as pl
from jax.experimental.pallas import tpu as pltpu
from jax.sharding import PartitionSpec as P

AXES = ("slab", "pen")
CHUNK = 32
BOX_X = 8
LANES = CHUNK * BOX_X
TILE = 8
SLOTS = TILE * CHUNK
f32 = jnp.float32
bf16 = jnp.bfloat16


def halves(table):
    high = table.astype(ml_dtypes.bfloat16)
    low = (table - high.astype(np.float64)).astype(ml_dtypes.bfloat16)
    return high, low


def split(value):
    high = value.astype(bf16)
    return high, (value - high.astype(f32)).astype(bf16)


def dot(a, b):
    return jnp.dot(a, b, preferred_element_type=f32)


def dot_nt(a, b):
    return lax.dot_general(a, b, (((1,), (1,)), ((), ())), preferred_element_type=f32)


def dot_tn(a, b):
    return lax.dot_general(a, b, (((0,), (0,)), ((), ())), preferred_element_type=f32)


def dot3(a_high, a_low, b_high, b_low, mul=dot):
    return mul(a_high, b_high) + (mul(a_high, b_low) + mul(a_low, b_high))


def iota(shape, dim):
    return lax.broadcasted_iota(jnp.int32, shape, dim)


def ones_where(mask):
    return jnp.where(mask, 1.0, 0.0).astype(bf16)


def plan_kernel(z_boxes, meta_ref, rows_ref, sx_ref, yl_ref, xb_ref, cz_ref, pos_ref):
    blocks = rows_ref.shape[0]
    groups = blocks // 128
    tiles = sx_ref.shape[0] // TILE
    below = ones_where(iota((128, 128), 0) < iota((128, 128), 1))
    base = jnp.zeros((z_boxes, 128), f32)
    marks, before = [], []
    for g in range(groups):
        box_z = meta_ref[0:1, 128 * g : 128 * g + 128]
        mark = jnp.where(iota((z_boxes, 128), 0) == box_z.astype(jnp.int32), 1.0, 0.0)
        marks.append(mark)
        before.append(base + dot(mark.astype(bf16), below))
        base = base + jnp.sum(mark, axis=1, keepdims=True)
    used = (base.astype(jnp.int32) + (CHUNK - 1)) // CHUNK
    lower = ones_where(iota((z_boxes, z_boxes), 1) < iota((z_boxes, z_boxes), 0))
    start = dot(lower, used.astype(f32).astype(bf16))
    for g in range(groups):
        place = jnp.sum(marks[g] * (start * CHUNK + before[g]), axis=0, keepdims=True)
        pos_ref[0:1, 128 * g : 128 * g + 128] = place.astype(jnp.int32)
    end = start.astype(jnp.int32) + used
    for t in range(cz_ref.shape[1] // 128):
        lane = iota((z_boxes, 128), 1) + 128 * t
        passed = jnp.where(end <= lane, 1, 0)
        cz_ref[0:1, 128 * t : 128 * t + 128] = jnp.sum(passed, axis=0, keepdims=True)
    cz_ref[1:2, 0:128] = jnp.sum(used, axis=0, keepdims=True)
    keep = iota((128, LANES), 0) % BOX_X == iota((128, LANES), 1) % BOX_X

    def tile(t, carry):
        hot = ones_where(iota((SLOTS, blocks), 0) + SLOTS * t == pos_ref[0:1, :])
        ordered = dot(hot, rows_ref[...]).astype(bf16)
        meta = dot_nt(meta_ref[...].astype(bf16), hot)
        xb_ref[0:1, pl.ds(pl.multiple_of(SLOTS * t, SLOTS), SLOTS)] = meta[2:3].astype(jnp.int32)
        meta = meta.astype(bf16)
        for q in range(TILE):
            spread = ones_where(iota((SLOTS, LANES), 0) == CHUNK * q + iota((SLOTS, LANES), 1) // BOX_X)
            wide = jnp.where(keep, dot_tn(ordered, spread), 0.0)
            sx_ref[TILE * t + q] = jnp.sum(wide.reshape(16, BOX_X, LANES), axis=1)
            yl_ref[TILE * t + q] = dot(meta, spread)
        return carry

    lax.fori_loop(0, tiles, tile, 0)


def field_kernel(cz_ref, xb_ref, sx_ref, yl_ref, ty_ref, tx_ref, uh_ref, ul_ref, ih_ref, il_ref, kh_ref, out_ref, grid_ref, cols_ref, ex_ref):
    depth, cv, _ = grid_ref.shape
    nv = cv // 2
    nw = kh_ref.shape[3]
    freqs = kh_ref.shape[2]
    y_boxes = ty_ref.shape[1] // 2
    total = cz_ref[1, 0]

    def clear(z, carry):
        grid_ref[z] = jnp.zeros((cv, 2 * nw), f32)
        return carry

    lax.fori_loop(0, depth, clear, 0)

    def wipe(c, carry):
        out_ref[c] = jnp.zeros((16, LANES), f32)
        return carry

    lax.fori_loop(total, out_ref.shape[0], wipe, 0)

    def tables(c):
        for b in range(CHUNK):
            ex_ref[BOX_X * b : BOX_X * b + BOX_X, :] = tx_ref[xb_ref[0, CHUNK * c + b]]
        hot = ones_where(iota((y_boxes, LANES), 0) == yl_ref[c][1:2].astype(jnp.int32))
        along = dot(ty_ref[...], jnp.concatenate([hot, hot], axis=0))
        return split(ex_ref[...]), along

    def scatter(c, carry):
        (ex_high, ex_low), along = tables(c)
        box = sx_ref[c]
        parts = []
        for i in range(4):
            part = along[0:cv] * box[4 * i : 4 * i + 1]
            for j in range(1, 4):
                part = part + along[cv * j : cv * j + cv] * box[4 * i + j : 4 * i + j + 1]
            parts.append(part)
        high, low = split(jnp.concatenate(parts, axis=0))
        added = dot3(high, low, ex_high, ex_low).reshape(4, cv, 2 * nw)
        where = pl.ds(4 * cz_ref[0, c], 4)
        grid_ref[where] = grid_ref[where] + added
        return carry

    lax.fori_loop(0, total, scatter, 0)

    def to_columns(g, carry):
        rows = pl.ds(pl.multiple_of(8 * g, 8), 8)
        for z in range(depth // 8):
            piece = grid_ref[8 * z : 8 * z + 8, rows, :]
            cols_ref[rows, 8 * z : 8 * z + 8, :] = jnp.swapaxes(piece, 0, 1)
        return carry

    lax.fori_loop(0, cv // 8, to_columns, 0)

    def column(p, carry):
        real, imag = [], []
        for v in (2 * p, 2 * p + 1):
            re, im = cols_ref[v], cols_ref[nv + v]
            real.append(re[:, :nw] - im[:, nw:])
            imag.append(re[:, nw:] + im[:, :nw])
        field = jnp.concatenate([jnp.concatenate(real, axis=1), jnp.concatenate(imag, axis=1)], axis=0)
        high, low = split(field)
        spec = dot3(uh_ref[...], ul_ref[...], high, low)
        k_re = jnp.concatenate([kh_ref[2 * p, 0], kh_ref[2 * p + 1, 0]], axis=1)
        k_im = jnp.concatenate([kh_ref[2 * p, 1], kh_ref[2 * p + 1, 1]], axis=1)
        s_re, s_im = spec[:freqs], spec[freqs:]
        prod = jnp.concatenate([k_re * s_re - k_im * s_im, k_re * s_im + k_im * s_re], axis=0)
        high, low = split(prod)
        back = dot3(ih_ref[...], il_ref[...], high, low)
        for n in range(2):
            q_re = back[:depth, nw * n : nw * n + nw]
            q_im = back[depth:, nw * n : nw * n + nw]
            cols_ref[2 * p + n] = jnp.concatenate([q_re, q_im], axis=1)
            cols_ref[nv + 2 * p + n] = jnp.concatenate([q_im, -q_re], axis=1)
        return carry

    lax.fori_loop(0, nv // 2, column, 0)

    def to_planes(g, carry):
        rows = pl.ds(pl.multiple_of(8 * g, 8), 8)
        for z in range(depth // 8):
            piece = cols_ref[rows, 8 * z : 8 * z + 8, :]
            grid_ref[8 * z : 8 * z + 8, rows, :] = jnp.swapaxes(piece, 0, 1)
        return carry

    lax.fori_loop(0, cv // 8, to_planes, 0)

    def gather(c, carry):
        (ex_high, ex_low), along = tables(c)
        planes = grid_ref[pl.ds(4 * cz_ref[0, c], 4)].reshape(4 * cv, 2 * nw)
        high, low = split(planes)
        lines = dot3(high, low, ex_high, ex_low, dot_nt)
        rows = []
        for i in range(4):
            for j in range(4):
                rows.append(jnp.sum(along[cv * j : cv * j + cv] * lines[cv * i : cv * i + cv], axis=0, keepdims=True))
        out_ref[c] = jnp.concatenate(rows, axis=0)
        return carry

    lax.fori_loop(0, total, gather, 0)


def unsort_kernel(got_ref, pos_ref, out_ref, acc_ref):
    blocks = pos_ref.shape[1]
    tiles = got_ref.shape[0] // TILE
    keep = iota((128, LANES), 0) % BOX_X == iota((128, LANES), 1) % BOX_X
    repeat = ones_where(iota((128, 16), 0) // BOX_X == iota((128, 16), 1))
    acc_ref[...] = jnp.zeros_like(acc_ref)

    def tile(t, carry):
        rows = jnp.zeros((128, SLOTS), f32)
        for q in range(TILE):
            wide = jnp.where(keep, dot(repeat, got_ref[TILE * t + q].astype(bf16)), 0.0).astype(bf16)
            pick = ones_where(CHUNK * q + iota((LANES, SLOTS), 0) // BOX_X == iota((LANES, SLOTS), 1))
            rows = rows + dot(wide, pick)
        hot = ones_where(iota((SLOTS, blocks), 0) + SLOTS * t == pos_ref[0:1, :])
        acc_ref[...] += dot(rows.astype(bf16), hot)
        return carry

    lax.fori_loop(0, tiles, tile, 0)
    for g in range(blocks // 128):
        out_ref[128 * g : 128 * g + 128, :] = acc_ref[:, 128 * g : 128 * g + 128].T.astype(bf16)


def turn(length, steps):
    angle = 2.0 * math.pi * (steps % length) / length
    return np.cos(angle), np.sin(angle)


def shards(charges, counts, proj_weight, dest_slab, box_index, pair_target, pair_source, near_matrix, kernel_hat):
    blocks, slots = charges.shape
    stencil = proj_weight.shape[2]
    slab_count = lax.axis_size("slab")
    pen_count = lax.axis_size("pen")
    devices = slab_count * pen_count
    freqs, nv, nw = kernel_hat.shape[1:]
    depth = freqs // 2
    width_y = nv * slab_count
    width_x = nw * pen_count
    planes = freqs // slab_count
    rows_pen = width_y // pen_count
    total_blocks = blocks * devices
    z_boxes, y_boxes, x_boxes = depth // 4, width_y // 4, width_x // BOX_X
    chunks = -(-(total_blocks // CHUNK + z_boxes) // TILE) * TILE
    factor = 1.0 / math.sqrt(float(freqs) * width_y * width_x * total_blocks * stencil)
    slab, pen = lax.axis_index("slab"), lax.axis_index("pen")

    live = jnp.arange(slots, dtype=jnp.int32)[None, :] < counts[:, None]
    charge = jnp.where(live, charges, jnp.zeros_like(charges))
    spread = jnp.einsum("bp,bps->bs", charge, proj_weight, preferred_element_type=f32)

    per_plane = rows_pen // 4 * x_boxes
    box_z = dest_slab[:, 0] * (planes // 4) + box_index // per_plane
    box_y = pen * (rows_pen // 4) + box_index // x_boxes % (rows_pen // 4)
    box_x = box_index % x_boxes
    meta = jnp.stack([box_z, box_y, box_x]).astype(bf16)
    meta = jnp.pad(meta, ((0, 5), (0, stencil - blocks)))
    packet = jnp.concatenate([spread.astype(bf16), meta], axis=0)
    packets = lax.all_to_all(jnp.broadcast_to(packet, (devices,) + packet.shape), AXES, 0, 0, tiled=True)
    rows = packets[:, :blocks].reshape(total_blocks, stencil)
    boxes = packets[:, blocks:, :blocks].transpose(1, 0, 2).reshape(8, total_blocks).astype(f32)

    lane_tiles = -(-chunks // 128) * 128
    plan = pl.pallas_call(
        functools.partial(plan_kernel, z_boxes),
        out_shape=(
            jax.ShapeDtypeStruct((chunks, 16, LANES), f32),
            jax.ShapeDtypeStruct((chunks, 8, LANES), f32),
            jax.ShapeDtypeStruct((1, chunks * CHUNK), jnp.int32),
            jax.ShapeDtypeStruct((2, lane_tiles), jnp.int32),
            jax.ShapeDtypeStruct((1, total_blocks), jnp.int32),
        ),
        compiler_params=pltpu.CompilerParams(vmem_limit_bytes=48 << 20),
        name="plan",
    )
    sx, yl, xb, cz, pos = plan(boxes, rows)

    v_all, yb_all = np.arange(width_y), np.arange(y_boxes)
    cos, sin = turn(width_y, v_all[None, :, None] * (4 * yb_all[None, None, :] + np.arange(4)[:, None, None]))
    high, low = halves(np.stack([cos, -sin], axis=1))
    along = np.concatenate([high, low], axis=3)
    ty = lax.dynamic_slice_in_dim(jnp.asarray(along), slab * nv, nv, 2).reshape(8 * nv, 2 * y_boxes)

    x_all = jnp.arange(width_x, dtype=jnp.int32)[:, None]
    w_own = pen * nw + jnp.arange(nw, dtype=jnp.int32)[None, :]
    phase = (x_all * w_own % width_x).astype(f32) * (2.0 * math.pi / width_x)
    tx = jnp.concatenate([jnp.cos(phase), -jnp.sin(phase)], axis=1).reshape(x_boxes, BOX_X, 2 * nw)

    cos, sin = turn(freqs, np.arange(freqs)[:, None] * np.arange(depth)[None, :])
    forth = np.block([[cos, sin], [-sin, cos]])
    uh, ul = halves(forth)
    ih, il = halves(forth.T * factor)
    kh = jnp.transpose(kernel_hat, (2, 0, 1, 3))

    vmem = pl.BlockSpec(memory_space=pltpu.VMEM)
    smem = pl.BlockSpec(memory_space=pltpu.SMEM)
    field = pl.pallas_call(
        field_kernel,
        out_shape=jax.ShapeDtypeStruct((chunks, 16, LANES), f32),
        in_specs=[smem, smem] + [vmem] * 9,
        out_specs=vmem,
        scratch_shapes=[
            pltpu.VMEM((depth, 2 * nv, 2 * nw), f32),
            pltpu.VMEM((2 * nv, depth, 2 * nw), f32),
            pltpu.VMEM((LANES, 2 * nw), f32),
        ],
        compiler_params=pltpu.CompilerParams(vmem_limit_bytes=56 << 20),
        name="field",
    )
    got = field(cz, xb, sx, yl, ty, tx, jnp.asarray(uh), jnp.asarray(ul), jnp.asarray(ih), jnp.asarray(il), kh)
    unsort = pl.pallas_call(
        unsort_kernel,
        out_shape=jax.ShapeDtypeStruct((total_blocks, stencil), bf16),
        scratch_shapes=[pltpu.VMEM((stencil, total_blocks), f32)],
        compiler_params=pltpu.CompilerParams(vmem_limit_bytes=48 << 20),
        name="unsort",
    )
    partial = unsort(got, pos)
    shares = lax.all_to_all(partial.reshape(devices, blocks, stencil), AXES, 0, 0, tiled=True)
    samples = jnp.sum(shares.astype(f32), axis=0).astype(bf16)

    far = jnp.einsum("bps,bs->bp", proj_weight, samples, preferred_element_type=f32)
    driven = charge[pair_source]
    terms = jnp.einsum("tpq,tq->tp", near_matrix, driven, preferred_element_type=f32)
    owners = (pair_target[:, None] == jnp.arange(blocks, dtype=jnp.int32)[None, :]).astype(f32)
    near = jnp.einsum("tb,tp->bp", owners, terms, precision=lax.Precision.HIGHEST)
    total = jnp.where(live, far + near, jnp.zeros_like(far))
    return total.astype(bf16)


def solution(mesh):
    placed = (
        P(AXES, None),
        P(AXES),
        P(AXES, None, None),
        P(AXES, None),
        P(AXES),
        P(AXES),
        P(AXES),
        P(AXES, None, None),
        P(None, None, "slab", "pen"),
    )
    return jax.shard_map(shards, mesh=mesh, in_specs=placed, out_specs=P(AXES, None), check_vma=False)
```

```python
import functools
import math

import jax
import jax.numpy as jnp
import ml_dtypes
import numpy as np
from jax import lax
from jax.experimental import pallas as pl
from jax.experimental.pallas import tpu as pltpu
from jax.sharding import PartitionSpec as P

AXES = ("slab", "pen")
CHUNK = 32
BOX_X = 8
LANES = CHUNK * BOX_X
TILE = 8
SLOTS = TILE * CHUNK
f32 = jnp.float32
bf16 = jnp.bfloat16


def halves(table):
    high = table.astype(ml_dtypes.bfloat16)
    low = (table - high.astype(np.float64)).astype(ml_dtypes.bfloat16)
    return high, low


def split(value):
    high = value.astype(bf16)
    return high, (value - high.astype(f32)).astype(bf16)


def dot(a, b):
    return jnp.dot(a, b, preferred_element_type=f32)


def dot_nt(a, b):
    return lax.dot_general(a, b, (((1,), (1,)), ((), ())), preferred_element_type=f32)


def dot_tn(a, b):
    return lax.dot_general(a, b, (((0,), (0,)), ((), ())), preferred_element_type=f32)


def dot3(a_high, a_low, b_high, b_low, mul=dot):
    return mul(a_high, b_high) + (mul(a_high, b_low) + mul(a_low, b_high))


def iota(shape, dim):
    return lax.broadcasted_iota(jnp.int32, shape, dim)


def ones_where(mask):
    return jnp.where(mask, 1.0, 0.0).astype(bf16)


def farm_kernel(
    keep, half, flag_ref, meta_ref, rows_ref, ty_ref, tx_ref, uh_ref, ul_ref, ih_ref, il_ref, kernel_ref,
    out_ref, grid_ref, cols_ref, edge_ref, ex_ref, eh_ref, el_ref, along_ref, kh_ref, sx_ref, yl_ref, got_ref, acc_ref,
    place_ref, boxes_ref, index_ref, cz_ref, xb_ref, kernel_sems, index_sems,
):
    depth, cv, _ = grid_ref.shape
    z_boxes = depth // 4
    nv = cv // 2
    nw = kh_ref.shape[3]
    freqs = kh_ref.shape[2]
    y_boxes = ty_ref.shape[1] // 2
    blocks = rows_ref.shape[0]
    groups = blocks // 128

    copies = []
    for v in range(nv + 1):
        source = 0 if v == nv else 2 * v + flag_ref[0, 0] if half else v
        for part in range(2):
            copies.append(pltpu.make_async_copy(kernel_ref.at[part, :, source, :], kh_ref.at[v, part], kernel_sems.at[v, part]))
    for copy in copies:
        copy.start()

    below = ones_where(iota((128, 128), 0) < iota((128, 128), 1))
    base = jnp.zeros((z_boxes, 128), f32)
    marks, before = [], []
    for g in range(groups):
        box_z = meta_ref[0:1, 128 * g : 128 * g + 128]
        mark = jnp.where(iota((z_boxes, 128), 0) == box_z.astype(jnp.int32), 1.0, 0.0)
        marks.append(mark)
        before.append(base + dot(mark.astype(bf16), below))
        base = base + jnp.sum(mark, axis=1, keepdims=True)
    used = (base.astype(jnp.int32) + (CHUNK - 1)) // CHUNK
    lower = ones_where(iota((z_boxes, z_boxes), 1) < iota((z_boxes, z_boxes), 0))
    start = dot(lower, used.astype(f32).astype(bf16))
    for g in range(groups):
        place = jnp.sum(marks[g] * (start * CHUNK + before[g]), axis=0, keepdims=True)
        place_ref[0:1, 128 * g : 128 * g + 128] = place.astype(jnp.int32)
    end = start.astype(jnp.int32) + used
    for t in range(boxes_ref.shape[1] // 128):
        lane = iota((z_boxes, 128), 1) + 128 * t
        passed = jnp.where(end <= lane, 1, 0)
        boxes_ref[0:1, 128 * t : 128 * t + 128] = jnp.sum(passed, axis=0, keepdims=True)
    boxes_ref[1:2, 0:128] = jnp.sum(used, axis=0, keepdims=True)
    copy = pltpu.make_async_copy(boxes_ref, cz_ref, index_sems.at[0])
    copy.start()
    copy.wait()
    steps = (cz_ref[1, 0] + 1) // 2
    tiles = (2 * steps + TILE - 1) // TILE
    same = iota((128, LANES), 0) % BOX_X == iota((128, LANES), 1) % BOX_X
    wide_of = ones_where(iota((CHUNK, LANES), 0) == iota((CHUNK, LANES), 1) // BOX_X)

    def sort(t, carry):
        hot = ones_where(iota((SLOTS, blocks), 0) + SLOTS * t == place_ref[0:1, :])
        ordered = dot(hot, rows_ref[...]).astype(bf16)
        meta = dot_nt(meta_ref[...].astype(bf16), hot)
        index_ref[0:1, pl.ds(pl.multiple_of(SLOTS * t, SLOTS), SLOTS)] = meta[2:3].astype(jnp.int32)
        meta = meta.astype(bf16)
        for q in range(TILE):
            own = slice(CHUNK * q, CHUNK * q + CHUNK)
            wide = jnp.where(same, dot_tn(ordered[own], wide_of), 0.0)
            sx_ref[TILE * t + q] = jnp.sum(wide.reshape(16, BOX_X, LANES), axis=1)
            yl_ref[TILE * t + q] = dot(meta[:, own], wide_of)
        return carry

    lax.fori_loop(0, tiles, sort, 0)
    copy = pltpu.make_async_copy(index_ref, xb_ref, index_sems.at[1])
    copy.start()
    copy.wait()

    def clear(z, carry):
        grid_ref[z] = jnp.zeros((cv, 2 * nw), f32)
        return carry

    lax.fori_loop(0, depth, clear, 0)
    edge_ref[...] = jnp.zeros_like(edge_ref)

    def tables(c, n):
        for b in range(CHUNK):
            ex_ref[n, BOX_X * b : BOX_X * b + BOX_X, :] = tx_ref[xb_ref[0, CHUNK * c + b]]
        hot = ones_where(iota((y_boxes, LANES), 0) == yl_ref[c][1:2].astype(jnp.int32))
        along = dot(ty_ref[...], jnp.concatenate([hot, hot], axis=0))
        return split(ex_ref[n]), along

    def box_of(c):
        return jnp.minimum(cz_ref[0, c], depth // 4 - 1)

    def scatter(step, carry):
        for n in range(2):
            c = 2 * step + n
            (ex_high, ex_low), along = tables(c, n)
            if keep:
                eh_ref[c], el_ref[c], along_ref[c] = ex_high, ex_low, along
            box = sx_ref[c]
            parts, edges = [], []
            for i in range(4):
                line = [box[4 * i + j : 4 * i + j + 1] for j in range(4)]
                part = along[0:cv] * line[0]
                for j in range(1, 4):
                    part = part + along[cv * j : cv * j + cv] * line[j]
                parts.append(part)
                edges.append((line[0] - line[1]) + (line[2] - line[3]))
            edges.append(jnp.zeros((4, LANES), f32))
            high, low = split(jnp.concatenate(parts + edges, axis=0))
            added = dot3(high, low, ex_high, ex_low)
            where = pl.ds(4 * box_of(c), 4)
            grid_ref[where] = grid_ref[where] + added[: 4 * cv].reshape(4, cv, 2 * nw)
            edge_ref[box_of(c)] = edge_ref[box_of(c)] + added[4 * cv :]
        return carry

    lax.fori_loop(0, steps, scatter, 0)

    def to_columns(g, carry):
        rows = pl.ds(pl.multiple_of(8 * g, 8), 8)
        for z in range(depth // 8):
            piece = grid_ref[8 * z : 8 * z + 8, rows, :]
            cols_ref[rows, 8 * z : 8 * z + 8, :] = jnp.swapaxes(piece, 0, 1)
        return carry

    lax.fori_loop(0, cv // 8, to_columns, 0)

    def filtered(real, imag, kernels):
        field = jnp.concatenate([jnp.concatenate(real, axis=1), jnp.concatenate(imag, axis=1)], axis=0)
        high, low = split(field)
        spec = dot3(uh_ref[...], ul_ref[...], high, low)
        k_re = jnp.concatenate([kh_ref[v, 0] for v in kernels], axis=1)
        k_im = jnp.concatenate([kh_ref[v, 1] for v in kernels], axis=1)
        s_re, s_im = spec[:freqs], spec[freqs:]
        prod = jnp.concatenate([k_re * s_re - k_im * s_im, k_re * s_im + k_im * s_re], axis=0)
        high, low = split(prod)
        back = dot3(ih_ref[...], il_ref[...], high, low)
        return back[:depth], back[depth:]

    def column(p, carry):
        real, imag = [], []
        for v in (2 * p, 2 * p + 1):
            re, im = cols_ref[v], cols_ref[nv + v]
            real.append(re[:, :nw] - im[:, nw:])
            imag.append(re[:, nw:] + im[:, :nw])
        q_re, q_im = filtered(real, imag, (2 * p, 2 * p + 1))
        for n in range(2):
            part = slice(nw * n, nw * n + nw)
            cols_ref[2 * p + n] = jnp.concatenate([q_re[:, part], q_im[:, part]], axis=1)
            cols_ref[nv + 2 * p + n] = jnp.concatenate([q_im[:, part], -q_re[:, part]], axis=1)
        return carry

    for copy in copies:
        copy.wait()
    lax.fori_loop(0, nv // 2, column, 0)

    edge = jnp.concatenate([edge_ref[z][0:4] for z in range(depth // 4)], axis=0)
    q_re, q_im = filtered([edge[:, :nw]], [edge[:, nw:]], (nv,))
    edge = jnp.concatenate([q_re, q_im], axis=1) * flag_ref[0, 1].astype(f32)
    for z in range(depth // 4):
        edge_ref[z, 0:4, :] = edge[4 * z : 4 * z + 4]

    def to_planes(g, carry):
        rows = pl.ds(pl.multiple_of(8 * g, 8), 8)
        for z in range(depth // 8):
            piece = cols_ref[rows, 8 * z : 8 * z + 8, :]
            grid_ref[8 * z : 8 * z + 8, rows, :] = jnp.swapaxes(piece, 0, 1)
        return carry

    lax.fori_loop(0, cv // 8, to_planes, 0)

    def gather(step, carry):
        for n in range(2):
            c = 2 * step + n
            if keep:
                ex_high, ex_low, along = eh_ref[c], el_ref[c], along_ref[c]
            else:
                (ex_high, ex_low), along = tables(c, n)
            planes = grid_ref[pl.ds(4 * box_of(c), 4)].reshape(4 * cv, 2 * nw)
            high, low = split(jnp.concatenate([planes, edge_ref[box_of(c)]], axis=0))
            lines = dot3(high, low, ex_high, ex_low, dot_nt)
            rows = []
            for i in range(4):
                edge = lines[4 * cv + i : 4 * cv + i + 1]
                for j in range(4):
                    row = jnp.sum(along[cv * j : cv * j + cv] * lines[cv * i : cv * i + cv], axis=0, keepdims=True)
                    rows.append(row - edge if j % 2 else row + edge)
            got_ref[c] = jnp.concatenate(rows, axis=0).astype(bf16)
        return carry

    lax.fori_loop(0, steps, gather, 0)

    repeat = ones_where(iota((128, 16), 0) // BOX_X == iota((128, 16), 1))
    acc_ref[...] = jnp.zeros_like(acc_ref)

    def wipe(c, carry):
        got_ref[c] = jnp.zeros((16, LANES), bf16)
        return carry

    lax.fori_loop(2 * steps, TILE * tiles, wipe, 0)

    def unsort(t, carry):
        rows = []
        for q in range(TILE):
            wide = jnp.where(same, dot(repeat, got_ref[TILE * t + q]), 0.0).astype(bf16)
            rows.append(dot_nt(wide_of, wide))
        rows = jnp.concatenate(rows, axis=0).astype(bf16)
        hot = ones_where(iota((SLOTS, blocks), 0) + SLOTS * t == place_ref[0:1, :])
        acc_ref[...] += dot_tn(rows, hot)
        return carry

    lax.fori_loop(0, tiles, unsort, 0)
    for g in range(groups):
        out_ref[128 * g : 128 * g + 128, :] = acc_ref[:, 128 * g : 128 * g + 128].T.astype(bf16)


def turn(length, steps):
    angle = 2.0 * math.pi * (steps % length) / length
    return np.cos(angle), np.sin(angle)


def shards(charges, counts, proj_weight, dest_slab, box_index, pair_target, pair_source, near_matrix, kernel_hat):
    blocks, slots = charges.shape
    stencil = proj_weight.shape[2]
    slab_count = lax.axis_size("slab")
    pen_count = lax.axis_size("pen")
    devices = slab_count * pen_count
    freqs, nv, nw = kernel_hat.shape[1:]
    depth = freqs // 2
    width_y = nv * slab_count
    width_x = nw * pen_count
    planes = freqs // slab_count
    rows_pen = width_y // pen_count
    total_blocks = blocks * devices
    z_boxes, y_boxes, x_boxes = depth // 4, width_y // 4, width_x // BOX_X
    chunks = -(-(total_blocks // CHUNK + z_boxes) // TILE) * TILE
    factor = 1.0 / math.sqrt(float(freqs) * width_y * width_x * total_blocks * stencil)
    slab, pen = lax.axis_index("slab"), lax.axis_index("pen")

    live = jnp.arange(slots, dtype=jnp.int32)[None, :] < counts[:, None]
    charge = jnp.where(live, charges, jnp.zeros_like(charges))
    spread = jnp.einsum("bp,bps->bs", charge, proj_weight, preferred_element_type=f32)

    per_plane = rows_pen // 4 * x_boxes
    box_z = dest_slab[:, 0] * (planes // 4) + box_index // per_plane
    box_y = pen * (rows_pen // 4) + box_index // x_boxes % (rows_pen // 4)
    box_x = box_index % x_boxes
    meta = jnp.stack([box_z, box_y, box_x]).astype(bf16)
    meta = jnp.pad(meta, ((0, 5), (0, stencil - blocks)))
    packet = jnp.concatenate([spread.astype(bf16), meta], axis=0)
    packets = lax.all_to_all(jnp.broadcast_to(packet, (devices,) + packet.shape), AXES, 0, 0, tiled=True)
    rows = packets[:, :blocks].reshape(total_blocks, stencil)
    boxes = packets[:, blocks:, :blocks].transpose(1, 0, 2).reshape(8, total_blocks).astype(f32)

    v_all, yb_all = np.arange(width_y), np.arange(y_boxes)
    cos, sin = turn(width_y, v_all[None, :, None] * (4 * yb_all[None, None, :] + np.arange(4)[:, None, None]))
    half = nv % 8 == 0
    scale = np.where((v_all == 0) | (not half), 1.0, math.sqrt(2.0))[None, :, None]
    high, low = halves(np.stack([cos * scale, -sin * scale], axis=1))
    along = np.concatenate([high, low], axis=3)
    odd = slab >= slab_count // 2
    own = nv // 2 if half else nv
    if half:
        along = jnp.where(odd, jnp.asarray(along[:, :, 1::2]), jnp.asarray(along[:, :, 0::2]))
    ty = lax.dynamic_slice_in_dim(jnp.asarray(along), slab * own, own, 2).reshape(8 * own, 2 * y_boxes)

    x_all = jnp.arange(width_x, dtype=jnp.int32)[:, None]
    w_own = pen * nw + jnp.arange(nw, dtype=jnp.int32)[None, :]
    phase = (x_all * w_own % width_x).astype(f32) * (2.0 * math.pi / width_x)
    tx = jnp.concatenate([jnp.cos(phase), -jnp.sin(phase)], axis=1).reshape(x_boxes, BOX_X, 2 * nw)

    cos, sin = turn(freqs, np.arange(freqs)[:, None] * np.arange(depth)[None, :])
    forth = np.block([[cos, sin], [-sin, cos]])
    uh, ul = halves(forth)
    ih, il = halves(forth.T * factor)
    last = jnp.logical_and(half, slab == slab_count // 2)
    flags = jnp.stack([odd, last]).astype(jnp.int32)[None, :]
    keep = chunks <= 64
    kept = chunks if keep else 1
    vmem = pl.BlockSpec(memory_space=pltpu.VMEM)
    smem = pl.BlockSpec(memory_space=pltpu.SMEM)
    lane_tiles = -(-chunks // 128) * 128
    farm = pl.pallas_call(
        functools.partial(farm_kernel, keep, half),
        out_shape=jax.ShapeDtypeStruct((total_blocks, stencil), bf16),
        in_specs=[smem] + [vmem] * 8 + [pl.BlockSpec(memory_space=pl.ANY)],
        out_specs=vmem,
        scratch_shapes=[
            pltpu.VMEM((depth, 2 * own, 2 * nw), f32),
            pltpu.VMEM((2 * own, depth, 2 * nw), f32),
            pltpu.VMEM((z_boxes, 8, 2 * nw), f32),
            pltpu.VMEM((2, LANES, 2 * nw), f32),
            pltpu.VMEM((kept, LANES, 2 * nw), bf16),
            pltpu.VMEM((kept, LANES, 2 * nw), bf16),
            pltpu.VMEM((kept, 8 * own, LANES), f32),
            pltpu.VMEM((own + 1, 2, freqs, nw), f32),
            pltpu.VMEM((chunks, 16, LANES), f32),
            pltpu.VMEM((chunks, 8, LANES), f32),
            pltpu.VMEM((chunks, 16, LANES), bf16),
            pltpu.VMEM((stencil, total_blocks), f32),
            pltpu.VMEM((1, total_blocks), jnp.int32),
            pltpu.VMEM((2, lane_tiles), jnp.int32),
            pltpu.VMEM((1, chunks * CHUNK), jnp.int32),
            pltpu.SMEM((2, lane_tiles), jnp.int32),
            pltpu.SMEM((1, chunks * CHUNK), jnp.int32),
            pltpu.SemaphoreType.DMA((own + 1, 2)),
            pltpu.SemaphoreType.DMA((2,)),
        ],
        compiler_params=pltpu.CompilerParams(vmem_limit_bytes=58 << 20),
        name="farm",
    )
    partial = farm(flags, boxes, rows, ty, tx, jnp.asarray(uh), jnp.asarray(ul), jnp.asarray(ih), jnp.asarray(il), kernel_hat)
    shares = lax.all_to_all(partial.reshape(devices, blocks, stencil), AXES, 0, 0, tiled=True)
    samples = jnp.sum(shares.astype(f32), axis=0).astype(bf16)

    far = jnp.einsum("bps,bs->bp", proj_weight, samples, preferred_element_type=f32)
    driven = charge[pair_source]
    terms = jnp.einsum("tpq,tq->tp", near_matrix, driven, preferred_element_type=f32)
    owners = (pair_target[:, None] == jnp.arange(blocks, dtype=jnp.int32)[None, :]).astype(f32)
    near = jnp.einsum("tb,tp->bp", owners, terms, precision=lax.Precision.HIGHEST)
    total = jnp.where(live, far + near, jnp.zeros_like(far))
    return total.astype(bf16)


def solution(mesh):
    placed = (
        P(AXES, None),
        P(AXES),
        P(AXES, None, None),
        P(AXES, None),
        P(AXES),
        P(AXES),
        P(AXES),
        P(AXES, None, None),
        P(None, None, "slab", "pen"),
    )
    return jax.shard_map(shards, mesh=mesh, in_specs=placed, out_specs=P(AXES, None), check_vma=False)
```

```python
import functools
import math

import jax
import jax.numpy as jnp
import ml_dtypes
import numpy as np
from jax import lax
from jax.experimental import pallas as pl
from jax.experimental.pallas import tpu as pltpu
from jax.sharding import PartitionSpec as P

AXES = ("slab", "pen")
CHUNK = 32
BOX_X = 8
LANES = CHUNK * BOX_X
TILE = 8
SLOTS = TILE * CHUNK
f32 = jnp.float32
bf16 = jnp.bfloat16


def halves(table):
    high = table.astype(ml_dtypes.bfloat16)
    low = (table - high.astype(np.float64)).astype(ml_dtypes.bfloat16)
    return high, low


def split(value):
    high = value.astype(bf16)
    return high, (value - high.astype(f32)).astype(bf16)


def dot(a, b):
    return jnp.dot(a, b, preferred_element_type=f32)


def dot_nt(a, b):
    return lax.dot_general(a, b, (((1,), (1,)), ((), ())), preferred_element_type=f32)


def dot_tn(a, b):
    return lax.dot_general(a, b, (((0,), (0,)), ((), ())), preferred_element_type=f32)


def dot3(a_high, a_low, b_high, b_low):
    left = jnp.concatenate([a_high, a_high, a_low], axis=1)
    return dot(left, jnp.concatenate([b_high, b_low, b_high], axis=0))


def stacked(mul, a_high, a_low, b_high, b_low):
    rows = a_high.shape[0]
    both = mul(jnp.concatenate([a_high, a_low], axis=0), b_high)
    return both[:rows] + (both[rows:] + mul(a_high, b_low))


def row_sums(parts):
    order = [parts[n] for n in (0, 4, 2, 6, 1, 5, 3, 7)]
    for step in (4, 2, 1):
        first = iota(order[0].shape, 0) % (2 * step) < step
        merged = []
        for a, b in zip(order[0::2], order[1::2]):
            kept = jnp.where(first, a, b)
            moved = jnp.where(first, b, a)
            merged.append(kept + (pltpu.roll(moved, 4, 0) if step == 4 else swap_rows(moved, step, first)))
        order = merged
    return order[0]


def swap_rows(value, step, first):
    return jnp.where(first, pltpu.roll(value, 8 - step, 0), pltpu.roll(value, step, 0))


def iota(shape, dim):
    return lax.broadcasted_iota(jnp.int32, shape, dim)


def ones_where(mask):
    return jnp.where(mask, 1.0, 0.0).astype(bf16)


def farm_kernel(
    keep, half, flag_ref, meta_ref, rows_ref, ty_ref, tx_ref, uh_ref, ul_ref, ih_ref, il_ref, kernel_ref,
    out_ref, grid_ref, cols_ref, edge_ref, ex_ref, eh_ref, el_ref, along_ref, kh_ref, sx_ref, yl_ref, got_ref, acc_ref,
    place_ref, boxes_ref, index_ref, cz_ref, xb_ref, kernel_sems, index_sems,
):
    depth, cv, _ = grid_ref.shape
    z_boxes = depth // 4
    nv = cv // 2
    nw = kh_ref.shape[3]
    freqs = kh_ref.shape[2]
    y_boxes = ty_ref.shape[1] // 2
    blocks = rows_ref.shape[0]
    groups = blocks // 128

    copies = []
    for v in range(nv + 1):
        source = 0 if v == nv else 2 * v + flag_ref[0, 0] if half else v
        for part in range(2):
            copies.append(pltpu.make_async_copy(kernel_ref.at[part, :, source, :], kh_ref.at[v, part], kernel_sems.at[v, part]))
    for copy in copies:
        copy.start()

    below = ones_where(iota((128, 128), 0) < iota((128, 128), 1))
    base = jnp.zeros((z_boxes, 128), f32)
    marks, before = [], []
    for g in range(groups):
        box_z = meta_ref[0:1, 128 * g : 128 * g + 128]
        mark = jnp.where(iota((z_boxes, 128), 0) == box_z.astype(jnp.int32), 1.0, 0.0)
        marks.append(mark)
        before.append(base + dot(mark.astype(bf16), below))
        base = base + jnp.sum(mark, axis=1, keepdims=True)
    used = (base.astype(jnp.int32) + (CHUNK - 1)) // CHUNK
    lower = ones_where(iota((z_boxes, z_boxes), 1) < iota((z_boxes, z_boxes), 0))
    start = dot(lower, used.astype(f32).astype(bf16))
    for g in range(groups):
        place = jnp.sum(marks[g] * (start * CHUNK + before[g]), axis=0, keepdims=True)
        place_ref[0:1, 128 * g : 128 * g + 128] = place.astype(jnp.int32)
    end = start.astype(jnp.int32) + used
    for t in range(boxes_ref.shape[1] // 128):
        lane = iota((z_boxes, 128), 1) + 128 * t
        passed = jnp.where(end <= lane, 1, 0)
        boxes_ref[0:1, 128 * t : 128 * t + 128] = jnp.sum(passed, axis=0, keepdims=True)
    boxes_ref[1:2, 0:128] = jnp.sum(used, axis=0, keepdims=True)
    copy = pltpu.make_async_copy(boxes_ref, cz_ref, index_sems.at[0])
    copy.start()
    copy.wait()
    steps = (cz_ref[1, 0] + 1) // 2
    tiles = (2 * steps + TILE - 1) // TILE
    row, col = iota((LANES, LANES), 0), iota((LANES, LANES), 1)
    to_lanes = ones_where((row // CHUNK == col % BOX_X) & (row % CHUNK == col // BOX_X))
    from_lanes = ones_where((col // CHUNK == row % BOX_X) & (col % CHUNK == row // BOX_X))
    row, col = iota((128, 128), 0), iota((128, 128), 1)
    points_first = ones_where((row // 16 == col % BOX_X) & (row % 16 == col // BOX_X))

    def sort(t, carry):
        hot = ones_where(iota((SLOTS, blocks), 0) + SLOTS * t == place_ref[0:1, :])
        ordered = dot(hot, rows_ref[...]).astype(bf16)
        turned = dot_nt(points_first, ordered)
        lines = exchanged([turned[16 * k : 16 * k + 16] for k in range(BOX_X)])
        lines = dot(jnp.concatenate(lines, axis=0).astype(bf16), to_lanes)
        sx_ref[pl.ds(TILE * t, TILE)] = lines.reshape(TILE, 16, LANES)
        meta = dot_nt(meta_ref[...].astype(bf16), hot)
        index_ref[0:1, pl.ds(pl.multiple_of(SLOTS * t, SLOTS), SLOTS)] = meta[2:3].astype(jnp.int32)
        owned = jnp.where(iota((TILE, SLOTS), 1) // CHUNK == iota((TILE, SLOTS), 0), meta[1:2], 0.0)
        owned = owned[:, :128] + owned[:, 128:]
        owned = owned + pltpu.roll(owned, 64, 1)
        owned = owned + pltpu.roll(owned, 32, 1)
        owned = jnp.concatenate([owned, owned], axis=1).astype(bf16)
        yl_ref[pl.ds(pl.multiple_of(TILE * t, TILE), TILE), :] = dot(owned, to_lanes)
        return carry

    lax.fori_loop(0, tiles, sort, 0)
    copy = pltpu.make_async_copy(index_ref, xb_ref, index_sems.at[1])
    copy.start()
    copy.wait()

    def clear(z, carry):
        grid_ref[z] = jnp.zeros((cv, 2 * nw), f32)
        return carry

    lax.fori_loop(0, depth, clear, 0)
    edge_ref[...] = jnp.zeros_like(edge_ref)

    def tables(c, n):
        for b in range(CHUNK):
            ex_ref[n, BOX_X * b : BOX_X * b + BOX_X, :] = tx_ref[xb_ref[0, CHUNK * c + b]]
        hot = ones_where(iota((y_boxes, LANES), 0) == yl_ref[pl.ds(c, 1), :].astype(jnp.int32))
        along = dot(ty_ref[...], jnp.concatenate([hot, hot], axis=0))
        return split(ex_ref[n]), along

    def box_of(c):
        return jnp.minimum(cz_ref[0, c], depth // 4 - 1)

    def scatter(step, carry):
        for n in range(2):
            c = 2 * step + n
            (ex_high, ex_low), along = tables(c, n)
            if keep:
                eh_ref[c], el_ref[c], along_ref[c] = ex_high, ex_low, along
            box = sx_ref[c]
            parts, edges = [], []
            for i in range(4):
                line = [box[4 * i + j : 4 * i + j + 1] for j in range(4)]
                part = along[0:cv] * line[0]
                for j in range(1, 4):
                    part = part + along[cv * j : cv * j + cv] * line[j]
                parts.append(part)
                edges.append((line[0] - line[1]) + (line[2] - line[3]))
            edges.append(jnp.zeros((4, LANES), f32))
            high, low = split(jnp.concatenate(parts + edges, axis=0))
            added = stacked(dot, high, low, ex_high, ex_low)
            where = pl.ds(4 * box_of(c), 4)
            grid_ref[where] = grid_ref[where] + added[: 4 * cv].reshape(4, cv, 2 * nw)
            edge_ref[box_of(c)] = edge_ref[box_of(c)] + added[4 * cv :]
        return carry

    lax.fori_loop(0, steps, scatter, 0)

    def to_columns(g, carry):
        rows = pl.ds(pl.multiple_of(8 * g, 8), 8)
        for z in range(depth // 8):
            piece = grid_ref[8 * z : 8 * z + 8, rows, :]
            cols_ref[rows, 8 * z : 8 * z + 8, :] = jnp.swapaxes(piece, 0, 1)
        return carry

    lax.fori_loop(0, cv // 8, to_columns, 0)

    def filtered(real, imag, kernels):
        field = jnp.concatenate([jnp.concatenate(real, axis=1), jnp.concatenate(imag, axis=1)], axis=0)
        high, low = split(field)
        spec = dot3(uh_ref[...], ul_ref[...], high, low)
        k_re = jnp.concatenate([kh_ref[v, 0] for v in kernels], axis=1)
        k_im = jnp.concatenate([kh_ref[v, 1] for v in kernels], axis=1)
        s_re, s_im = spec[:freqs], spec[freqs:]
        prod = jnp.concatenate([k_re * s_re - k_im * s_im, k_re * s_im + k_im * s_re], axis=0)
        high, low = split(prod)
        back = dot3(ih_ref[...], il_ref[...], high, low)
        return back[:depth], back[depth:]

    def column(step, carry):
        for p in (2 * step, 2 * step + 1):
            real, imag = [], []
            for v in (2 * p, 2 * p + 1):
                re, im = cols_ref[v], cols_ref[nv + v]
                real.append(re[:, :nw] - im[:, nw:])
                imag.append(re[:, nw:] + im[:, :nw])
            q_re, q_im = filtered(real, imag, (2 * p, 2 * p + 1))
            for n in range(2):
                part = slice(nw * n, nw * n + nw)
                cols_ref[2 * p + n] = jnp.concatenate([q_re[:, part], q_im[:, part]], axis=1)
                cols_ref[nv + 2 * p + n] = jnp.concatenate([q_im[:, part], -q_re[:, part]], axis=1)
        return carry

    for copy in copies:
        copy.wait()
    lax.fori_loop(0, nv // 4, column, 0)

    edge = jnp.concatenate([edge_ref[z][0:4] for z in range(depth // 4)], axis=0)
    q_re, q_im = filtered([edge[:, :nw]], [edge[:, nw:]], (nv,))
    edge = jnp.concatenate([q_re, q_im], axis=1) * flag_ref[0, 1].astype(f32)
    for z in range(depth // 4):
        edge_ref[z, 0:4, :] = edge[4 * z : 4 * z + 4]

    def to_planes(g, carry):
        rows = pl.ds(pl.multiple_of(8 * g, 8), 8)
        for z in range(depth // 8):
            piece = cols_ref[rows, 8 * z : 8 * z + 8, :]
            grid_ref[8 * z : 8 * z + 8, rows, :] = jnp.swapaxes(piece, 0, 1)
        return carry

    lax.fori_loop(0, cv // 8, to_planes, 0)

    def gather(step, carry):
        for n in range(2):
            c = 2 * step + n
            if keep:
                ex_high, ex_low, along = eh_ref[c], el_ref[c], along_ref[c]
            else:
                (ex_high, ex_low), along = tables(c, n)
            planes = grid_ref[pl.ds(4 * box_of(c), 4)].reshape(4 * cv, 2 * nw)
            high, low = split(jnp.concatenate([planes, edge_ref[box_of(c)]], axis=0))
            lines = stacked(dot_nt, high, low, ex_high, ex_low)
            got = []
            for i in (0, 2):
                parts = []
                for n in range(8):
                    at, j = i + n // 4, n % 4
                    part = along[cv * j : cv * j + cv] * lines[cv * at : cv * at + cv]
                    parts.append(jnp.sum(part.reshape(cv // 8, 8, LANES), axis=0))
                first = lines[4 * cv + i : 4 * cv + i + 1]
                second = lines[4 * cv + i + 1 : 4 * cv + i + 2]
                edge = jnp.where(iota((8, LANES), 0) < 4, first, second)
                edge = jnp.where(iota((8, LANES), 0) % 2 == 0, edge, -edge)
                got.append(row_sums(parts) + edge)
            got_ref[c] = jnp.concatenate(got, axis=0).astype(bf16)
        return carry

    lax.fori_loop(0, steps, gather, 0)

    acc_ref[...] = jnp.zeros_like(acc_ref)

    def wipe(c, carry):
        got_ref[c] = jnp.zeros((16, LANES), bf16)
        return carry

    lax.fori_loop(2 * steps, TILE * tiles, wipe, 0)

    def unsort(t, carry):
        lines = got_ref[pl.ds(TILE * t, TILE)].reshape(TILE * 16, LANES)
        lines = dot(lines, from_lanes)
        rows = exchanged([lines[16 * q : 16 * q + 16] for q in range(TILE)])
        hot = ones_where(iota((SLOTS, blocks), 0) + SLOTS * t == place_ref[0:1, :])
        acc_ref[...] += dot(jnp.concatenate(rows, axis=0).astype(bf16), hot)
        return carry

    lax.fori_loop(0, tiles, unsort, 0)
    for g in range(groups):
        part = acc_ref[:, 128 * g : 128 * g + 128].astype(bf16)
        out_ref[128 * g : 128 * g + 128, :] = dot_tn(part, points_first).astype(bf16)


def exchanged(lines):
    lane = iota((16, 128), 1) // CHUNK
    results = []
    for q in range(8):
        tiles = []
        for h in range(2):
            tile = None
            for a in range(4):
                piece = lines[4 * h + a][:, 128 * (q // 4) : 128 * (q // 4) + 128]
                shift = CHUNK * (a - q % 4) % 128
                piece = pltpu.roll(piece, shift, 1) if shift else piece
                tile = piece if tile is None else jnp.where(lane == a, piece, tile)
            tiles.append(tile)
        results.append(jnp.concatenate(tiles, axis=1))
    return results


def turn(length, steps):
    angle = 2.0 * math.pi * (steps % length) / length
    return np.cos(angle), np.sin(angle)


def shards(charges, counts, proj_weight, dest_slab, box_index, pair_target, pair_source, near_matrix, kernel_hat):
    blocks, slots = charges.shape
    stencil = proj_weight.shape[2]
    slab_count = lax.axis_size("slab")
    pen_count = lax.axis_size("pen")
    devices = slab_count * pen_count
    freqs, nv, nw = kernel_hat.shape[1:]
    depth = freqs // 2
    width_y = nv * slab_count
    width_x = nw * pen_count
    planes = freqs // slab_count
    rows_pen = width_y // pen_count
    total_blocks = blocks * devices
    z_boxes, y_boxes, x_boxes = depth // 4, width_y // 4, width_x // BOX_X
    chunks = -(-(total_blocks // CHUNK + z_boxes) // TILE) * TILE
    factor = 1.0 / math.sqrt(float(freqs) * width_y * width_x * total_blocks * stencil)
    slab, pen = lax.axis_index("slab"), lax.axis_index("pen")

    live = jnp.arange(slots, dtype=jnp.int32)[None, :] < counts[:, None]
    charge = jnp.where(live, charges, jnp.zeros_like(charges))
    spread = jnp.einsum("bp,bps->bs", charge, proj_weight, preferred_element_type=f32)

    per_plane = rows_pen // 4 * x_boxes
    box_z = dest_slab[:, 0] * (planes // 4) + box_index // per_plane
    box_y = pen * (rows_pen // 4) + box_index // x_boxes % (rows_pen // 4)
    box_x = box_index % x_boxes
    meta = jnp.stack([box_z, box_y, box_x]).astype(bf16)
    meta = jnp.pad(meta, ((0, 5), (0, stencil - blocks)))
    packet = jnp.concatenate([spread.astype(bf16), meta], axis=0)
    packets = lax.all_to_all(jnp.broadcast_to(packet, (devices,) + packet.shape), AXES, 0, 0, tiled=True)
    rows = packets[:, :blocks].reshape(total_blocks, stencil)
    boxes = packets[:, blocks:, :blocks].transpose(1, 0, 2).reshape(8, total_blocks).astype(f32)

    v_all, yb_all = np.arange(width_y), np.arange(y_boxes)
    cos, sin = turn(width_y, v_all[None, :, None] * (4 * yb_all[None, None, :] + np.arange(4)[:, None, None]))
    half = nv % 8 == 0
    scale = np.where((v_all == 0) | (not half), 1.0, math.sqrt(2.0))[None, :, None]
    high, low = halves(np.stack([cos * scale, -sin * scale], axis=1))
    along = np.concatenate([high, low], axis=3)
    odd = slab >= slab_count // 2
    own = nv // 2 if half else nv
    if half:
        along = jnp.where(odd, jnp.asarray(along[:, :, 1::2]), jnp.asarray(along[:, :, 0::2]))
    ty = lax.dynamic_slice_in_dim(jnp.asarray(along), slab * own, own, 2).reshape(8 * own, 2 * y_boxes)

    x_all = jnp.arange(width_x, dtype=jnp.int32)[:, None]
    w_own = pen * nw + jnp.arange(nw, dtype=jnp.int32)[None, :]
    phase = (x_all * w_own % width_x).astype(f32) * (2.0 * math.pi / width_x)
    tx = jnp.concatenate([jnp.cos(phase), -jnp.sin(phase)], axis=1).reshape(x_boxes, BOX_X, 2 * nw)

    cos, sin = turn(freqs, np.arange(freqs)[:, None] * np.arange(depth)[None, :])
    forth = np.block([[cos, sin], [-sin, cos]])
    uh, ul = halves(forth)
    ih, il = halves(forth.T * factor)
    last = jnp.logical_and(half, slab == slab_count // 2)
    flags = jnp.stack([odd, last]).astype(jnp.int32)[None, :]
    keep = chunks <= 64
    kept = chunks if keep else 1
    vmem = pl.BlockSpec(memory_space=pltpu.VMEM)
    smem = pl.BlockSpec(memory_space=pltpu.SMEM)
    lane_tiles = -(-chunks // 128) * 128
    farm = pl.pallas_call(
        functools.partial(farm_kernel, keep, half),
        out_shape=jax.ShapeDtypeStruct((total_blocks, stencil), bf16),
        in_specs=[smem] + [vmem] * 8 + [pl.BlockSpec(memory_space=pl.ANY)],
        out_specs=vmem,
        scratch_shapes=[
            pltpu.VMEM((depth, 2 * own, 2 * nw), f32),
            pltpu.VMEM((2 * own, depth, 2 * nw), f32),
            pltpu.VMEM((z_boxes, 8, 2 * nw), f32),
            pltpu.VMEM((2, LANES, 2 * nw), f32),
            pltpu.VMEM((kept, LANES, 2 * nw), bf16),
            pltpu.VMEM((kept, LANES, 2 * nw), bf16),
            pltpu.VMEM((kept, 8 * own, LANES), f32),
            pltpu.VMEM((own + 1, 2, freqs, nw), f32),
            pltpu.VMEM((chunks, 16, LANES), f32),
            pltpu.VMEM((chunks, LANES), f32),
            pltpu.VMEM((chunks, 16, LANES), bf16),
            pltpu.VMEM((stencil, total_blocks), f32),
            pltpu.VMEM((1, total_blocks), jnp.int32),
            pltpu.VMEM((2, lane_tiles), jnp.int32),
            pltpu.VMEM((1, chunks * CHUNK), jnp.int32),
            pltpu.SMEM((2, lane_tiles), jnp.int32),
            pltpu.SMEM((1, chunks * CHUNK), jnp.int32),
            pltpu.SemaphoreType.DMA((own + 1, 2)),
            pltpu.SemaphoreType.DMA((2,)),
        ],
        compiler_params=pltpu.CompilerParams(vmem_limit_bytes=58 << 20),
        name="farm",
    )
    partial = farm(flags, boxes, rows, ty, tx, jnp.asarray(uh), jnp.asarray(ul), jnp.asarray(ih), jnp.asarray(il), kernel_hat)
    shares = lax.all_to_all(partial.reshape(devices, blocks, stencil), AXES, 0, 0, tiled=True)
    samples = jnp.sum(shares.astype(f32), axis=0).astype(bf16)

    far = jnp.einsum("bps,bs->bp", proj_weight, samples, preferred_element_type=f32)
    driven = charge[pair_source]
    terms = jnp.einsum("tpq,tq->tp", near_matrix, driven, preferred_element_type=f32)
    owners = (pair_target[:, None] == jnp.arange(blocks, dtype=jnp.int32)[None, :]).astype(f32)
    near = jnp.einsum("tb,tp->bp", owners, terms, precision=lax.Precision.HIGHEST)
    total = jnp.where(live, far + near, jnp.zeros_like(far))
    return total.astype(bf16)


def solution(mesh):
    placed = (
        P(AXES, None),
        P(AXES),
        P(AXES, None, None),
        P(AXES, None),
        P(AXES),
        P(AXES),
        P(AXES),
        P(AXES, None, None),
        P(None, None, "slab", "pen"),
    )
    return jax.shard_map(shards, mesh=mesh, in_specs=placed, out_specs=P(AXES, None), check_vma=False)
```

```python
import functools
import math

import jax
import jax.numpy as jnp
import ml_dtypes
import numpy as np
from jax import lax
from jax.experimental import pallas as pl
from jax.experimental.pallas import tpu as pltpu
from jax.sharding import PartitionSpec as P

AXES = ("slab", "pen")
CHUNK = 32
BOX_X = 8
LANES = CHUNK * BOX_X
UNROLL = 4
TILE = 8
SLOTS = TILE * CHUNK
f32 = jnp.float32
bf16 = jnp.bfloat16


def halves(table):
    high = table.astype(ml_dtypes.bfloat16)
    low = (table - high.astype(np.float64)).astype(ml_dtypes.bfloat16)
    return high, low


def split(value):
    high = value.astype(bf16)
    return high, (value - high.astype(f32)).astype(bf16)


def dot(a, b):
    return jnp.dot(a, b, preferred_element_type=f32)


def dot_nt(a, b):
    return lax.dot_general(a, b, (((1,), (1,)), ((), ())), preferred_element_type=f32)


def dot_tn(a, b):
    return lax.dot_general(a, b, (((0,), (0,)), ((), ())), preferred_element_type=f32)


def dot3(a_high, a_low, b_high, b_low):
    left = jnp.concatenate([a_high, a_high, a_low], axis=1)
    return dot(left, jnp.concatenate([b_high, b_low, b_high], axis=0))


def stacked(mul, a_high, a_low, b_high, b_low):
    rows = a_high.shape[0]
    both = mul(jnp.concatenate([a_high, a_low], axis=0), b_high)
    return both[:rows] + (both[rows:] + mul(a_high, b_low))


def row_sums(parts):
    order = [parts[n] for n in (0, 4, 2, 6, 1, 5, 3, 7)]
    for step in (4, 2, 1):
        first = iota(order[0].shape, 0) % (2 * step) < step
        merged = []
        for a, b in zip(order[0::2], order[1::2]):
            kept = jnp.where(first, a, b)
            moved = jnp.where(first, b, a)
            merged.append(kept + (pltpu.roll(moved, 4, 0) if step == 4 else swap_rows(moved, step, first)))
        order = merged
    return order[0]


def swap_rows(value, step, first):
    return jnp.where(first, pltpu.roll(value, 8 - step, 0), pltpu.roll(value, step, 0))


def iota(shape, dim):
    return lax.broadcasted_iota(jnp.int32, shape, dim)


def ones_where(mask):
    return jnp.where(mask, 1.0, 0.0).astype(bf16)


def pack_kernel(grid_shape, charge_ref, live_ref, weight_ref, slab_ref, index_ref, out_ref, packet_ref):
    slab_boxes, row_boxes, x_boxes = grid_shape
    blocks, slots = charge_ref.shape
    counts = jnp.where(iota((blocks, blocks), 0) == iota((blocks, blocks), 1), live_ref[...], 0)
    live = iota((blocks, slots), 1) < jnp.sum(counts, axis=1, keepdims=True)
    charge = jnp.where(live, charge_ref[...].astype(f32), 0.0).astype(bf16)
    for b in range(blocks):
        packet_ref[b : b + 1, :] = dot(charge, weight_ref[b])[b : b + 1]
    packet_ref[blocks : blocks + 8, :] = jnp.zeros((8, slots), f32)
    place, x = index_ref[...] // x_boxes, index_ref[...] % x_boxes
    box = (slab_ref[...] * slab_boxes + place // row_boxes, place % row_boxes, x)
    for n in range(3):
        packet_ref[blocks + n : blocks + n + 1, 0:blocks] = box[n].astype(f32)
    packet = packet_ref[...].astype(bf16)

    def copy(d, carry):
        out_ref[d] = packet
        return carry

    lax.fori_loop(0, out_ref.shape[0], copy, 0)


def farm_kernel(
    keep, half, pens, flag_ref, packets_ref, ty_ref, tx_ref, uh_ref, ul_ref, ih_ref, il_ref, kernel_ref,
    out_ref, grid_ref, cols_ref, edge_ref, ex_ref, eh_ref, el_ref, along_ref, kh_ref, sx_ref, yl_ref, got_ref, acc_ref,
    meta_ref, rows_ref, place_ref, boxes_ref, index_ref, cz_ref, xb_ref, kernel_sems, index_sems,
):
    depth, cv, _ = grid_ref.shape
    z_boxes = depth // 4
    nv = cv // 2
    nw = kh_ref.shape[3]
    freqs = kh_ref.shape[2]
    y_boxes = ty_ref.shape[1] // 2
    blocks = rows_ref.shape[0]
    groups = blocks // 128

    copies = []
    for v in range(nv + 1):
        source = 0 if v == nv else 2 * v + flag_ref[0, 0] if half else v
        for part in range(2):
            copies.append(pltpu.make_async_copy(kernel_ref.at[part, :, source, :], kh_ref.at[v, part], kernel_sems.at[v, part]))
    for copy in copies:
        copy.start()

    own = packets_ref.shape[1] - 8

    def unpack(g, carry):
        meta = jnp.zeros((8, 128), f32)
        for n in range(128 // own):
            d = 128 // own * g + n
            rows_ref[pl.ds(pl.multiple_of(own * d, own), own), :] = packets_ref[d, 0:own, :]
            shift = n % pens * (y_boxes // pens)
            shifted = (iota((8, 128), 0) == 1) & (iota((8, 128), 1) < own)
            part = packets_ref[d, own : own + 8, :].astype(f32) + jnp.where(shifted, float(shift), 0.0)
            meta = meta + (pltpu.roll(part, own * n, 1) if n else part)
        meta_ref[:, pl.ds(pl.multiple_of(128 * g, 128), 128)] = meta
        return carry

    lax.fori_loop(0, groups, unpack, 0)
    below = ones_where(iota((128, 128), 0) < iota((128, 128), 1))
    base = jnp.zeros((z_boxes, 128), f32)
    marks, before = [], []
    for g in range(groups):
        box_z = meta_ref[0:1, 128 * g : 128 * g + 128]
        mark = jnp.where(iota((z_boxes, 128), 0) == box_z.astype(jnp.int32), 1.0, 0.0)
        marks.append(mark)
        before.append(base + dot(mark.astype(bf16), below))
        base = base + jnp.sum(mark, axis=1, keepdims=True)
    used = (base.astype(jnp.int32) + (CHUNK - 1)) // CHUNK
    lower = ones_where(iota((z_boxes, z_boxes), 1) < iota((z_boxes, z_boxes), 0))
    start = dot(lower, used.astype(f32).astype(bf16))
    for g in range(groups):
        place = jnp.sum(marks[g] * (start * CHUNK + before[g]), axis=0, keepdims=True)
        place_ref[0:1, 128 * g : 128 * g + 128] = place.astype(jnp.int32)
    end = start.astype(jnp.int32) + used
    for t in range(boxes_ref.shape[1] // 128):
        lane = iota((z_boxes, 128), 1) + 128 * t
        passed = jnp.where(end <= lane, 1, 0)
        boxes_ref[0:1, 128 * t : 128 * t + 128] = jnp.sum(passed, axis=0, keepdims=True)
    boxes_ref[1:2, 0:128] = jnp.sum(used, axis=0, keepdims=True)
    copy = pltpu.make_async_copy(boxes_ref, cz_ref, index_sems.at[0])
    copy.start()
    copy.wait()
    steps = (cz_ref[1, 0] + (UNROLL - 1)) // UNROLL
    tiles = (UNROLL * steps + TILE - 1) // TILE
    row, col = iota((LANES, LANES), 0), iota((LANES, LANES), 1)
    to_lanes = ones_where((row // CHUNK == col % BOX_X) & (row % CHUNK == col // BOX_X))
    from_lanes = ones_where((col // CHUNK == row % BOX_X) & (col % CHUNK == row // BOX_X))
    row, col = iota((128, 128), 0), iota((128, 128), 1)
    points_first = ones_where((row // 16 == col % BOX_X) & (row % 16 == col // BOX_X))

    def sort(t, carry):
        hot = ones_where(iota((SLOTS, blocks), 0) + SLOTS * t == place_ref[0:1, :])
        ordered = dot(hot, rows_ref[...]).astype(bf16)
        turned = dot_nt(points_first, ordered)
        lines = exchanged([turned[16 * k : 16 * k + 16] for k in range(BOX_X)])
        lines = dot(jnp.concatenate(lines, axis=0).astype(bf16), to_lanes)
        sx_ref[pl.ds(TILE * t, TILE)] = lines.reshape(TILE, 16, LANES)
        meta = dot_nt(meta_ref[...].astype(bf16), hot)
        index_ref[0:1, pl.ds(pl.multiple_of(SLOTS * t, SLOTS), SLOTS)] = meta[2:3].astype(jnp.int32)
        owned = jnp.where(iota((TILE, SLOTS), 1) // CHUNK == iota((TILE, SLOTS), 0), meta[1:2], 0.0)
        owned = owned[:, :128] + owned[:, 128:]
        owned = owned + pltpu.roll(owned, 64, 1)
        owned = owned + pltpu.roll(owned, 32, 1)
        owned = jnp.concatenate([owned, owned], axis=1).astype(bf16)
        yl_ref[pl.ds(pl.multiple_of(TILE * t, TILE), TILE), :] = dot(owned, to_lanes)
        return carry

    lax.fori_loop(0, tiles, sort, 0)
    copy = pltpu.make_async_copy(index_ref, xb_ref, index_sems.at[1])
    copy.start()
    copy.wait()

    def clear(z, carry):
        grid_ref[z] = jnp.zeros((cv, 2 * nw), f32)
        return carry

    lax.fori_loop(0, depth, clear, 0)
    edge_ref[...] = jnp.zeros_like(edge_ref)

    def tables(c, n):
        for b in range(CHUNK):
            ex_ref[n, BOX_X * b : BOX_X * b + BOX_X, :] = tx_ref[xb_ref[0, CHUNK * c + b]]
        hot = ones_where(iota((y_boxes, LANES), 0) == yl_ref[pl.ds(c, 1), :].astype(jnp.int32))
        along = dot(ty_ref[...], jnp.concatenate([hot, hot], axis=0))
        return split(ex_ref[n]), along

    def box_of(c):
        return jnp.minimum(cz_ref[0, c], depth // 4 - 1)

    def scatter(step, carry):
        for n in range(UNROLL):
            c = UNROLL * step + n
            (ex_high, ex_low), along = tables(c, n)
            if keep:
                eh_ref[c], el_ref[c], along_ref[c] = ex_high, ex_low, along
            box = sx_ref[c]
            parts, edges = [], []
            for i in range(4):
                line = [box[4 * i + j : 4 * i + j + 1] for j in range(4)]
                part = along[0:cv] * line[0]
                for j in range(1, 4):
                    part = part + along[cv * j : cv * j + cv] * line[j]
                parts.append(part)
                edges.append((line[0] - line[1]) + (line[2] - line[3]))
            edges.append(jnp.zeros((4, LANES), f32))
            high, low = split(jnp.concatenate(parts + edges, axis=0))
            added = dot3(high, low, ex_high, ex_low)
            where = pl.ds(4 * box_of(c), 4)
            grid_ref[where] = grid_ref[where] + added[: 4 * cv].reshape(4, cv, 2 * nw)
            edge_ref[box_of(c)] = edge_ref[box_of(c)] + added[4 * cv :]
        return carry

    lax.fori_loop(0, steps, scatter, 0)

    def to_columns(g, carry):
        rows = pl.ds(pl.multiple_of(8 * g, 8), 8)
        for z in range(depth // 8):
            piece = grid_ref[8 * z : 8 * z + 8, rows, :]
            cols_ref[rows, 8 * z : 8 * z + 8, :] = jnp.swapaxes(piece, 0, 1)
        return carry

    lax.fori_loop(0, cv // 8, to_columns, 0)

    def filtered(real, imag, kernels):
        field = jnp.concatenate([jnp.concatenate(real, axis=1), jnp.concatenate(imag, axis=1)], axis=0)
        high, low = split(field)
        spec = dot3(uh_ref[...], ul_ref[...], high, low)
        k_re = jnp.concatenate([kh_ref[v, 0] for v in kernels], axis=1)
        k_im = jnp.concatenate([kh_ref[v, 1] for v in kernels], axis=1)
        s_re, s_im = spec[:freqs], spec[freqs:]
        prod = jnp.concatenate([k_re * s_re - k_im * s_im, k_re * s_im + k_im * s_re], axis=0)
        high, low = split(prod)
        back = dot3(ih_ref[...], il_ref[...], high, low)
        return back[:depth], back[depth:]

    pairs = min(4, nv // 2)

    def column(step, carry):
        for p in [pairs * step + n for n in range(pairs)]:
            real, imag = [], []
            for v in (2 * p, 2 * p + 1):
                re, im = cols_ref[v], cols_ref[nv + v]
                real.append(re[:, :nw] - im[:, nw:])
                imag.append(re[:, nw:] + im[:, :nw])
            q_re, q_im = filtered(real, imag, (2 * p, 2 * p + 1))
            for n in range(2):
                part = slice(nw * n, nw * n + nw)
                cols_ref[2 * p + n] = jnp.concatenate([q_re[:, part], q_im[:, part]], axis=1)
                cols_ref[nv + 2 * p + n] = jnp.concatenate([q_im[:, part], -q_re[:, part]], axis=1)
        return carry

    for copy in copies:
        copy.wait()
    lax.fori_loop(0, nv // 2 // pairs, column, 0)

    edge = jnp.concatenate([edge_ref[z][0:4] for z in range(depth // 4)], axis=0)
    q_re, q_im = filtered([edge[:, :nw]], [edge[:, nw:]], (nv,))
    edge = jnp.concatenate([q_re, q_im], axis=1) * flag_ref[0, 1].astype(f32)
    for z in range(depth // 4):
        edge_ref[z, 0:4, :] = edge[4 * z : 4 * z + 4]

    def to_planes(g, carry):
        rows = pl.ds(pl.multiple_of(8 * g, 8), 8)
        for z in range(depth // 8):
            piece = cols_ref[rows, 8 * z : 8 * z + 8, :]
            grid_ref[8 * z : 8 * z + 8, rows, :] = jnp.swapaxes(piece, 0, 1)
        return carry

    lax.fori_loop(0, cv // 8, to_planes, 0)

    def gather(step, carry):
        for n in range(UNROLL):
            c = UNROLL * step + n
            if keep:
                ex_high, ex_low, along = eh_ref[c], el_ref[c], along_ref[c]
            else:
                (ex_high, ex_low), along = tables(c, n)
            planes = grid_ref[pl.ds(4 * box_of(c), 4)].reshape(4 * cv, 2 * nw)
            high, low = split(jnp.concatenate([planes, edge_ref[box_of(c)]], axis=0))
            lines = stacked(dot_nt, high, low, ex_high, ex_low)
            got = []
            for i in (0, 2):
                parts = []
                for n in range(8):
                    at, j = i + n // 4, n % 4
                    part = along[cv * j : cv * j + cv] * lines[cv * at : cv * at + cv]
                    parts.append(jnp.sum(part.reshape(cv // 8, 8, LANES), axis=0))
                first = lines[4 * cv + i : 4 * cv + i + 1]
                second = lines[4 * cv + i + 1 : 4 * cv + i + 2]
                edge = jnp.where(iota((8, LANES), 0) < 4, first, second)
                edge = jnp.where(iota((8, LANES), 0) % 2 == 0, edge, -edge)
                got.append(row_sums(parts) + edge)
            got_ref[c] = jnp.concatenate(got, axis=0).astype(bf16)
        return carry

    lax.fori_loop(0, steps, gather, 0)

    acc_ref[...] = jnp.zeros_like(acc_ref)

    def wipe(c, carry):
        got_ref[c] = jnp.zeros((16, LANES), bf16)
        return carry

    lax.fori_loop(UNROLL * steps, TILE * tiles, wipe, 0)

    def unsort(t, carry):
        lines = got_ref[pl.ds(TILE * t, TILE)].reshape(TILE * 16, LANES)
        lines = dot(lines, from_lanes)
        rows = exchanged([lines[16 * q : 16 * q + 16] for q in range(TILE)])
        hot = ones_where(iota((SLOTS, blocks), 0) + SLOTS * t == place_ref[0:1, :])
        acc_ref[...] += dot(jnp.concatenate(rows, axis=0).astype(bf16), hot)
        return carry

    lax.fori_loop(0, tiles, unsort, 0)
    for g in range(groups):
        part = acc_ref[:, 128 * g : 128 * g + 128].astype(bf16)
        out_ref[128 * g : 128 * g + 128, :] = dot_tn(part, points_first).astype(bf16)


def exchanged(lines):
    lane = iota((16, 128), 1) // CHUNK
    results = []
    for q in range(8):
        tiles = []
        for h in range(2):
            tile = None
            for a in range(4):
                piece = lines[4 * h + a][:, 128 * (q // 4) : 128 * (q // 4) + 128]
                shift = CHUNK * (a - q % 4) % 128
                piece = pltpu.roll(piece, shift, 1) if shift else piece
                tile = piece if tile is None else jnp.where(lane == a, piece, tile)
            tiles.append(tile)
        results.append(jnp.concatenate(tiles, axis=1))
    return results


def turn(length, steps):
    angle = 2.0 * math.pi * (steps % length) / length
    return np.cos(angle), np.sin(angle)


def shards(charges, counts, proj_weight, dest_slab, box_index, pair_target, pair_source, near_matrix, kernel_hat):
    blocks, slots = charges.shape
    stencil = proj_weight.shape[2]
    slab_count = lax.axis_size("slab")
    pen_count = lax.axis_size("pen")
    devices = slab_count * pen_count
    freqs, nv, nw = kernel_hat.shape[1:]
    depth = freqs // 2
    width_y = nv * slab_count
    width_x = nw * pen_count
    planes = freqs // slab_count
    rows_pen = width_y // pen_count
    total_blocks = blocks * devices
    z_boxes, y_boxes, x_boxes = depth // 4, width_y // 4, width_x // BOX_X
    chunks = -(-(total_blocks // CHUNK + z_boxes) // TILE) * TILE
    factor = 1.0 / math.sqrt(float(freqs) * width_y * width_x * total_blocks * stencil)
    slab, pen = lax.axis_index("slab"), lax.axis_index("pen")

    live = jnp.arange(slots, dtype=jnp.int32)[None, :] < counts[:, None]
    charge = jnp.where(live, charges, jnp.zeros_like(charges))
    vmem = pl.BlockSpec(memory_space=pltpu.VMEM)
    smem = pl.BlockSpec(memory_space=pltpu.SMEM)
    pack = pl.pallas_call(
        functools.partial(pack_kernel, (planes // 4, rows_pen // 4, x_boxes)),
        out_shape=jax.ShapeDtypeStruct((devices, blocks + 8, stencil), bf16),
        scratch_shapes=[pltpu.VMEM((blocks + 8, stencil), f32)],
        in_specs=[vmem] * 5,
        out_specs=vmem,
        name="pack",
    )
    packets = pack(charges, counts[None, :], proj_weight, dest_slab.reshape(1, blocks), box_index[None, :])
    packets = lax.all_to_all(packets, AXES, 0, 0, tiled=True)

    v_all, yb_all = np.arange(width_y), np.arange(y_boxes)
    cos, sin = turn(width_y, v_all[None, :, None] * (4 * yb_all[None, None, :] + np.arange(4)[:, None, None]))
    half = nv % 8 == 0
    scale = np.where((v_all == 0) | (not half), 1.0, math.sqrt(2.0))[None, :, None]
    high, low = halves(np.stack([cos * scale, -sin * scale], axis=1))
    along = np.concatenate([high, low], axis=3)
    odd = slab >= slab_count // 2
    own = nv // 2 if half else nv
    if half:
        along = jnp.where(odd, jnp.asarray(along[:, :, 1::2]), jnp.asarray(along[:, :, 0::2]))
    ty = lax.dynamic_slice_in_dim(jnp.asarray(along), slab * own, own, 2).reshape(8 * own, 2 * y_boxes)

    x_all = jnp.arange(width_x, dtype=jnp.int32)[:, None]
    w_own = pen * nw + jnp.arange(nw, dtype=jnp.int32)[None, :]
    phase = (x_all * w_own % width_x).astype(f32) * (2.0 * math.pi / width_x)
    tx = jnp.concatenate([jnp.cos(phase), -jnp.sin(phase)], axis=1).reshape(x_boxes, BOX_X, 2 * nw)

    cos, sin = turn(freqs, np.arange(freqs)[:, None] * np.arange(depth)[None, :])
    forth = np.block([[cos, sin], [-sin, cos]])
    uh, ul = halves(forth)
    ih, il = halves(forth.T * factor)
    last = jnp.logical_and(half, slab == slab_count // 2)
    flags = jnp.stack([odd, last]).astype(jnp.int32)[None, :]
    keep = chunks <= 64
    kept = chunks if keep else 1
    lane_tiles = -(-chunks // 128) * 128
    farm = pl.pallas_call(
        functools.partial(farm_kernel, keep, half, pen_count),
        out_shape=jax.ShapeDtypeStruct((total_blocks, stencil), bf16),
        in_specs=[smem] + [vmem] * 7 + [pl.BlockSpec(memory_space=pl.ANY)],
        out_specs=vmem,
        scratch_shapes=[
            pltpu.VMEM((depth, 2 * own, 2 * nw), f32),
            pltpu.VMEM((2 * own, depth, 2 * nw), f32),
            pltpu.VMEM((z_boxes, 8, 2 * nw), f32),
            pltpu.VMEM((UNROLL, LANES, 2 * nw), f32),
            pltpu.VMEM((kept, LANES, 2 * nw), bf16),
            pltpu.VMEM((kept, LANES, 2 * nw), bf16),
            pltpu.VMEM((kept, 8 * own, LANES), f32),
            pltpu.VMEM((own + 1, 2, freqs, nw), f32),
            pltpu.VMEM((chunks, 16, LANES), f32),
            pltpu.VMEM((chunks, LANES), f32),
            pltpu.VMEM((chunks, 16, LANES), bf16),
            pltpu.VMEM((stencil, total_blocks), f32),
            pltpu.VMEM((8, total_blocks), f32),
            pltpu.VMEM((total_blocks, stencil), bf16),
            pltpu.VMEM((1, total_blocks), jnp.int32),
            pltpu.VMEM((2, lane_tiles), jnp.int32),
            pltpu.VMEM((1, chunks * CHUNK), jnp.int32),
            pltpu.SMEM((2, lane_tiles), jnp.int32),
            pltpu.SMEM((1, chunks * CHUNK), jnp.int32),
            pltpu.SemaphoreType.DMA((own + 1, 2)),
            pltpu.SemaphoreType.DMA((2,)),
        ],
        compiler_params=pltpu.CompilerParams(vmem_limit_bytes=58 << 20),
        name="farm",
    )
    partial = farm(flags, packets, ty, tx, jnp.asarray(uh), jnp.asarray(ul), jnp.asarray(ih), jnp.asarray(il), kernel_hat)
    shares = lax.all_to_all(partial.reshape(devices, blocks, stencil), AXES, 0, 0, tiled=True)
    samples = jnp.sum(shares.astype(f32), axis=0).astype(bf16)

    far = jnp.einsum("bps,bs->bp", proj_weight, samples, preferred_element_type=f32)
    driven = charge[pair_source]
    terms = jnp.einsum("tpq,tq->tp", near_matrix, driven, preferred_element_type=f32)
    owners = (pair_target[:, None] == jnp.arange(blocks, dtype=jnp.int32)[None, :]).astype(f32)
    near = jnp.einsum("tb,tp->bp", owners, terms, precision=lax.Precision.HIGHEST)
    total = jnp.where(live, far + near, jnp.zeros_like(far))
    return total.astype(bf16)


def solution(mesh):
    placed = (
        P(AXES, None),
        P(AXES),
        P(AXES, None, None),
        P(AXES, None),
        P(AXES),
        P(AXES),
        P(AXES),
        P(AXES, None, None),
        P(None, None, "slab", "pen"),
    )
    return jax.shard_map(shards, mesh=mesh, in_specs=placed, out_specs=P(AXES, None), check_vma=False)
```

```python
import functools
import math

import jax
import jax.numpy as jnp
import ml_dtypes
import numpy as np
from jax import lax
from jax.experimental import pallas as pl
from jax.experimental.pallas import tpu as pltpu
from jax.sharding import PartitionSpec as P

AXES = ("slab", "pen")
CHUNK = 32
BOX_X = 8
LANES = CHUNK * BOX_X
UNROLL = 4
TILE = 8
SLOTS = TILE * CHUNK
f32 = jnp.float32
bf16 = jnp.bfloat16


def halves(table):
    high = table.astype(ml_dtypes.bfloat16)
    low = (table - high.astype(np.float64)).astype(ml_dtypes.bfloat16)
    return high, low


def split(value):
    high = value.astype(bf16)
    return high, (value - high.astype(f32)).astype(bf16)


def dot(a, b):
    return jnp.dot(a, b, preferred_element_type=f32)


def dot_nt(a, b):
    return lax.dot_general(a, b, (((1,), (1,)), ((), ())), preferred_element_type=f32)


def dot_tn(a, b):
    return lax.dot_general(a, b, (((0,), (0,)), ((), ())), preferred_element_type=f32)


def dot3(a_high, a_low, b_high, b_low):
    left = jnp.concatenate([a_high, a_high, a_low], axis=1)
    return dot(left, jnp.concatenate([b_high, b_low, b_high], axis=0))


def stacked(mul, a_high, a_low, b_high, b_low):
    rows = a_high.shape[0]
    both = mul(jnp.concatenate([a_high, a_low], axis=0), b_high)
    return both[:rows] + (both[rows:] + mul(a_high, b_low))


def row_sums(parts):
    order = [parts[n] for n in (0, 4, 2, 6, 1, 5, 3, 7)]
    for step in (4, 2, 1):
        first = iota(order[0].shape, 0) % (2 * step) < step
        merged = []
        for a, b in zip(order[0::2], order[1::2]):
            kept = jnp.where(first, a, b)
            moved = jnp.where(first, b, a)
            merged.append(kept + (pltpu.roll(moved, 4, 0) if step == 4 else swap_rows(moved, step, first)))
        order = merged
    return order[0]


def swap_rows(value, step, first):
    return jnp.where(first, pltpu.roll(value, 8 - step, 0), pltpu.roll(value, step, 0))


def iota(shape, dim):
    return lax.broadcasted_iota(jnp.int32, shape, dim)


def ones_where(mask):
    return jnp.where(mask, 1.0, 0.0).astype(bf16)


def pack_kernel(grid_shape, charge_ref, live_ref, weight_ref, slab_ref, index_ref, out_ref, packet_ref):
    slab_boxes, row_boxes, x_boxes = grid_shape
    blocks, slots = charge_ref.shape
    counts = jnp.where(iota((blocks, blocks), 0) == iota((blocks, blocks), 1), live_ref[...], 0)
    live = iota((blocks, slots), 1) < jnp.sum(counts, axis=1, keepdims=True)
    charge = jnp.where(live, charge_ref[...].astype(f32), 0.0).astype(bf16)
    for b in range(blocks):
        packet_ref[b : b + 1, :] = dot(charge, weight_ref[b])[b : b + 1]
    packet_ref[blocks : blocks + 8, :] = jnp.zeros((8, slots), f32)
    place, x = index_ref[...] // x_boxes, index_ref[...] % x_boxes
    box = (slab_ref[...] * slab_boxes + place // row_boxes, place % row_boxes, x)
    for n in range(3):
        packet_ref[blocks + n : blocks + n + 1, 0:blocks] = box[n].astype(f32)
    packet = packet_ref[...].astype(bf16)

    def copy(d, carry):
        out_ref[d] = packet
        return carry

    lax.fori_loop(0, out_ref.shape[0], copy, 0)


def farm_kernel(
    keep, half, pens, flag_ref, packets_ref, ty_ref, tx_ref, uh_ref, ul_ref, ih_ref, il_ref, kernel_ref,
    out_ref, grid_ref, cols_ref, edge_ref, ex_ref, eh_ref, el_ref, along_ref, kh_ref, sx_ref, yl_ref, got_ref, acc_ref, hot_ref,
    meta_ref, rows_ref, place_ref, boxes_ref, index_ref, cz_ref, xb_ref, kernel_sems, index_sems,
):
    depth, cv, _ = grid_ref.shape
    z_boxes = depth // 4
    nv = cv // 2
    nw = kh_ref.shape[3]
    freqs = kh_ref.shape[2]
    y_boxes = ty_ref.shape[1] // 2
    blocks = rows_ref.shape[0]
    groups = blocks // 128

    copies = []
    for v in range(nv + 1):
        source = 0 if v == nv else 2 * v + flag_ref[0, 0] if half else v
        for part in range(2):
            copies.append(pltpu.make_async_copy(kernel_ref.at[part, :, source, :], kh_ref.at[v, part], kernel_sems.at[v, part]))
    for copy in copies:
        copy.start()

    own = packets_ref.shape[1] - 8

    def unpack(g, carry):
        meta = jnp.zeros((8, 128), f32)
        for n in range(128 // own):
            d = 128 // own * g + n
            rows_ref[pl.ds(pl.multiple_of(own * d, own), own), :] = packets_ref[d, 0:own, :]
            shift = n % pens * (y_boxes // pens)
            shifted = (iota((8, 128), 0) == 1) & (iota((8, 128), 1) < own)
            part = packets_ref[d, own : own + 8, :].astype(f32) + jnp.where(shifted, float(shift), 0.0)
            meta = meta + (pltpu.roll(part, own * n, 1) if n else part)
        meta_ref[:, pl.ds(pl.multiple_of(128 * g, 128), 128)] = meta
        return carry

    lax.fori_loop(0, groups, unpack, 0, unroll=groups <= 8)
    below = ones_where(iota((128, 128), 0) < iota((128, 128), 1))
    base = jnp.zeros((z_boxes, 128), f32)
    marks, before = [], []
    for g in range(groups):
        box_z = meta_ref[0:1, 128 * g : 128 * g + 128]
        mark = jnp.where(iota((z_boxes, 128), 0) == box_z.astype(jnp.int32), 1.0, 0.0)
        marks.append(mark)
        before.append(base + dot(mark.astype(bf16), below))
        base = base + jnp.sum(mark, axis=1, keepdims=True)
    used = (base.astype(jnp.int32) + (CHUNK - 1)) // CHUNK
    lower = ones_where(iota((z_boxes, z_boxes), 1) < iota((z_boxes, z_boxes), 0))
    start = dot(lower, used.astype(f32).astype(bf16))
    for g in range(groups):
        place = jnp.sum(marks[g] * (start * CHUNK + before[g]), axis=0, keepdims=True)
        place_ref[0:1, 128 * g : 128 * g + 128] = place.astype(jnp.int32)
    end = start.astype(jnp.int32) + used
    for t in range(boxes_ref.shape[1] // 128):
        lane = iota((z_boxes, 128), 1) + 128 * t
        passed = jnp.where(end <= lane, 1, 0)
        boxes_ref[0:1, 128 * t : 128 * t + 128] = jnp.sum(passed, axis=0, keepdims=True)
    boxes_ref[1:2, 0:128] = jnp.sum(used, axis=0, keepdims=True)
    copy = pltpu.make_async_copy(boxes_ref, cz_ref, index_sems.at[0])
    copy.start()

    def clear(z, carry):
        grid_ref[z] = jnp.zeros((cv, 2 * nw), f32)
        return carry

    lax.fori_loop(0, depth, clear, 0)
    edge_ref[...] = jnp.zeros_like(edge_ref)
    copy.wait()
    steps = (cz_ref[1, 0] + (UNROLL - 1)) // UNROLL
    tiles = (UNROLL * steps + TILE - 1) // TILE
    row, col = iota((LANES, LANES), 0), iota((LANES, LANES), 1)
    to_lanes = ones_where((row // CHUNK == col % BOX_X) & (row % CHUNK == col // BOX_X))
    from_lanes = ones_where((col // CHUNK == row % BOX_X) & (col % CHUNK == row // BOX_X))
    row, col = iota((128, 128), 0), iota((128, 128), 1)
    points_first = ones_where((row // 16 == col % BOX_X) & (row % 16 == col // BOX_X))

    def sort(t, carry):
        hot = ones_where(iota((SLOTS, blocks), 0) + SLOTS * t == place_ref[0:1, :])
        if keep:
            hot_ref[t] = hot
        ordered = dot(hot, rows_ref[...]).astype(bf16)
        turned = dot_nt(points_first, ordered)
        lines = exchanged([turned[16 * k : 16 * k + 16] for k in range(BOX_X)])
        lines = dot(jnp.concatenate(lines, axis=0).astype(bf16), to_lanes)
        sx_ref[pl.ds(TILE * t, TILE)] = lines.reshape(TILE, 16, LANES)
        meta = dot_nt(meta_ref[...].astype(bf16), hot)
        index_ref[0:1, pl.ds(pl.multiple_of(SLOTS * t, SLOTS), SLOTS)] = meta[2:3].astype(jnp.int32)
        owned = jnp.where(iota((TILE, SLOTS), 1) // CHUNK == iota((TILE, SLOTS), 0), meta[1:2], 0.0)
        owned = owned[:, :128] + owned[:, 128:]
        owned = owned + pltpu.roll(owned, 64, 1)
        owned = owned + pltpu.roll(owned, 32, 1)
        owned = jnp.concatenate([owned, owned], axis=1).astype(bf16)
        yl_ref[pl.ds(pl.multiple_of(TILE * t, TILE), TILE), :] = dot(owned, to_lanes)
        return carry

    lax.fori_loop(0, tiles, sort, 0)
    copy = pltpu.make_async_copy(index_ref, xb_ref, index_sems.at[1])
    copy.start()
    copy.wait()

    def tables(c, n):
        for b in range(CHUNK):
            ex_ref[n, BOX_X * b : BOX_X * b + BOX_X, :] = tx_ref[xb_ref[0, CHUNK * c + b]]
        hot = ones_where(iota((y_boxes, LANES), 0) == yl_ref[pl.ds(c, 1), :].astype(jnp.int32))
        along = dot(ty_ref[...], jnp.concatenate([hot, hot], axis=0))
        return split(ex_ref[n]), along

    def box_of(c):
        return jnp.minimum(cz_ref[0, c], depth // 4 - 1)

    def scatter(step, carry):
        for n in range(UNROLL):
            c = UNROLL * step + n
            (ex_high, ex_low), along = tables(c, n)
            if keep:
                eh_ref[c], el_ref[c], along_ref[c] = ex_high, ex_low, along
            box = sx_ref[c]
            parts, edges = [], []
            for i in range(4):
                line = [box[4 * i + j : 4 * i + j + 1] for j in range(4)]
                part = along[0:cv] * line[0]
                for j in range(1, 4):
                    part = part + along[cv * j : cv * j + cv] * line[j]
                parts.append(part)
                edges.append((line[0] - line[1]) + (line[2] - line[3]))
            edges.append(jnp.zeros((4, LANES), f32))
            high, low = split(jnp.concatenate(parts + edges, axis=0))
            added = dot3(high, low, ex_high, ex_low)
            where = pl.ds(4 * box_of(c), 4)
            grid_ref[where] = grid_ref[where] + added[: 4 * cv].reshape(4, cv, 2 * nw)
            edge_ref[box_of(c)] = edge_ref[box_of(c)] + added[4 * cv :]
        return carry

    lax.fori_loop(0, steps, scatter, 0)

    def to_columns(g, carry):
        rows = pl.ds(pl.multiple_of(8 * g, 8), 8)
        for z in range(depth // 8):
            piece = grid_ref[8 * z : 8 * z + 8, rows, :]
            cols_ref[rows, 8 * z : 8 * z + 8, :] = jnp.swapaxes(piece, 0, 1)
        return carry

    lax.fori_loop(0, cv // 8, to_columns, 0)

    def filtered(real, imag, kernels):
        field = jnp.concatenate([jnp.concatenate(real, axis=1), jnp.concatenate(imag, axis=1)], axis=0)
        high, low = split(field)
        spec = dot3(uh_ref[...], ul_ref[...], high, low)
        k_re = jnp.concatenate([kh_ref[v, 0] for v in kernels], axis=1)
        k_im = jnp.concatenate([kh_ref[v, 1] for v in kernels], axis=1)
        s_re, s_im = spec[:freqs], spec[freqs:]
        prod = jnp.concatenate([k_re * s_re - k_im * s_im, k_re * s_im + k_im * s_re], axis=0)
        high, low = split(prod)
        back = dot3(ih_ref[...], il_ref[...], high, low)
        return back[:depth], back[depth:]

    pairs = min(4, nv // 2)

    def column(step, carry):
        for p in [pairs * step + n for n in range(pairs)]:
            real, imag = [], []
            for v in (2 * p, 2 * p + 1):
                re, im = cols_ref[v], cols_ref[nv + v]
                real.append(re[:, :nw] - im[:, nw:])
                imag.append(re[:, nw:] + im[:, :nw])
            q_re, q_im = filtered(real, imag, (2 * p, 2 * p + 1))
            for n in range(2):
                part = slice(nw * n, nw * n + nw)
                cols_ref[2 * p + n] = jnp.concatenate([q_re[:, part], q_im[:, part]], axis=1)
                cols_ref[nv + 2 * p + n] = jnp.concatenate([q_im[:, part], -q_re[:, part]], axis=1)
        return carry

    for copy in copies:
        copy.wait()
    lax.fori_loop(0, nv // 2 // pairs, column, 0)

    edge = jnp.concatenate([edge_ref[z][0:4] for z in range(depth // 4)], axis=0)
    q_re, q_im = filtered([edge[:, :nw]], [edge[:, nw:]], (nv,))
    edge = jnp.concatenate([q_re, q_im], axis=1) * flag_ref[0, 1].astype(f32)
    for z in range(depth // 4):
        edge_ref[z, 0:4, :] = edge[4 * z : 4 * z + 4]

    def to_planes(g, carry):
        rows = pl.ds(pl.multiple_of(8 * g, 8), 8)
        for z in range(depth // 8):
            piece = cols_ref[rows, 8 * z : 8 * z + 8, :]
            grid_ref[8 * z : 8 * z + 8, rows, :] = jnp.swapaxes(piece, 0, 1)
        return carry

    lax.fori_loop(0, cv // 8, to_planes, 0)

    def gather(step, carry):
        for n in range(UNROLL):
            c = UNROLL * step + n
            if keep:
                ex_high, ex_low, along = eh_ref[c], el_ref[c], along_ref[c]
            else:
                (ex_high, ex_low), along = tables(c, n)
            planes = grid_ref[pl.ds(4 * box_of(c), 4)].reshape(4 * cv, 2 * nw)
            high, low = split(jnp.concatenate([planes, edge_ref[box_of(c)]], axis=0))
            lines = stacked(dot_nt, high, low, ex_high, ex_low)
            got = []
            for i in (0, 2):
                parts = []
                for n in range(8):
                    at, j = i + n // 4, n % 4
                    part = along[cv * j : cv * j + cv] * lines[cv * at : cv * at + cv]
                    parts.append(jnp.sum(part.reshape(cv // 8, 8, LANES), axis=0))
                first = lines[4 * cv + i : 4 * cv + i + 1]
                second = lines[4 * cv + i + 1 : 4 * cv + i + 2]
                edge = jnp.where(iota((8, LANES), 0) < 4, first, second)
                edge = jnp.where(iota((8, LANES), 0) % 2 == 0, edge, -edge)
                got.append(row_sums(parts) + edge)
            got_ref[c] = jnp.concatenate(got, axis=0).astype(bf16)
        return carry

    lax.fori_loop(0, steps, gather, 0)

    acc_ref[...] = jnp.zeros_like(acc_ref)

    def wipe(c, carry):
        got_ref[c] = jnp.zeros((16, LANES), bf16)
        return carry

    lax.fori_loop(UNROLL * steps, TILE * tiles, wipe, 0)

    def unsort(t, carry):
        lines = got_ref[pl.ds(TILE * t, TILE)].reshape(TILE * 16, LANES)
        lines = dot(lines, from_lanes)
        rows = exchanged([lines[16 * q : 16 * q + 16] for q in range(TILE)])
        hot = hot_ref[t] if keep else ones_where(iota((SLOTS, blocks), 0) + SLOTS * t == place_ref[0:1, :])
        acc_ref[...] += dot(jnp.concatenate(rows, axis=0).astype(bf16), hot)
        return carry

    lax.fori_loop(0, tiles, unsort, 0)
    for g in range(groups):
        part = acc_ref[:, 128 * g : 128 * g + 128].astype(bf16)
        out_ref[128 * g : 128 * g + 128, :] = dot_tn(part, points_first).astype(bf16)


def exchanged(lines):
    lane = iota((16, 128), 1) // CHUNK
    results = []
    for q in range(8):
        tiles = []
        for h in range(2):
            tile = None
            for a in range(4):
                piece = lines[4 * h + a][:, 128 * (q // 4) : 128 * (q // 4) + 128]
                shift = CHUNK * (a - q % 4) % 128
                piece = pltpu.roll(piece, shift, 1) if shift else piece
                tile = piece if tile is None else jnp.where(lane == a, piece, tile)
            tiles.append(tile)
        results.append(jnp.concatenate(tiles, axis=1))
    return results


def turn(length, steps):
    angle = 2.0 * math.pi * (steps % length) / length
    return np.cos(angle), np.sin(angle)


def shards(charges, counts, proj_weight, dest_slab, box_index, pair_target, pair_source, near_matrix, kernel_hat):
    blocks, slots = charges.shape
    stencil = proj_weight.shape[2]
    slab_count = lax.axis_size("slab")
    pen_count = lax.axis_size("pen")
    devices = slab_count * pen_count
    freqs, nv, nw = kernel_hat.shape[1:]
    depth = freqs // 2
    width_y = nv * slab_count
    width_x = nw * pen_count
    planes = freqs // slab_count
    rows_pen = width_y // pen_count
    total_blocks = blocks * devices
    z_boxes, y_boxes, x_boxes = depth // 4, width_y // 4, width_x // BOX_X
    chunks = -(-(total_blocks // CHUNK + z_boxes) // TILE) * TILE
    factor = 1.0 / math.sqrt(float(freqs) * width_y * width_x * total_blocks * stencil)
    slab, pen = lax.axis_index("slab"), lax.axis_index("pen")

    live = jnp.arange(slots, dtype=jnp.int32)[None, :] < counts[:, None]
    charge = jnp.where(live, charges, jnp.zeros_like(charges))
    vmem = pl.BlockSpec(memory_space=pltpu.VMEM)
    smem = pl.BlockSpec(memory_space=pltpu.SMEM)
    pack = pl.pallas_call(
        functools.partial(pack_kernel, (planes // 4, rows_pen // 4, x_boxes)),
        out_shape=jax.ShapeDtypeStruct((devices, blocks + 8, stencil), bf16),
        scratch_shapes=[pltpu.VMEM((blocks + 8, stencil), f32)],
        in_specs=[vmem] * 5,
        out_specs=vmem,
        name="pack",
    )
    packets = pack(charges, counts[None, :], proj_weight, dest_slab.reshape(1, blocks), box_index[None, :])
    packets = lax.all_to_all(packets, AXES, 0, 0, tiled=True)

    v_all, yb_all = np.arange(width_y), np.arange(y_boxes)
    cos, sin = turn(width_y, v_all[None, :, None] * (4 * yb_all[None, None, :] + np.arange(4)[:, None, None]))
    half = nv % 8 == 0
    scale = np.where((v_all == 0) | (not half), 1.0, math.sqrt(2.0))[None, :, None]
    high, low = halves(np.stack([cos * scale, -sin * scale], axis=1))
    along = np.concatenate([high, low], axis=3)
    odd = slab >= slab_count // 2
    own = nv // 2 if half else nv
    if half:
        along = jnp.where(odd, jnp.asarray(along[:, :, 1::2]), jnp.asarray(along[:, :, 0::2]))
    ty = lax.dynamic_slice_in_dim(jnp.asarray(along), slab * own, own, 2).reshape(8 * own, 2 * y_boxes)

    x_all = jnp.arange(width_x, dtype=jnp.int32)[:, None]
    w_own = pen * nw + jnp.arange(nw, dtype=jnp.int32)[None, :]
    phase = (x_all * w_own % width_x).astype(f32) * (2.0 * math.pi / width_x)
    tx = jnp.concatenate([jnp.cos(phase), -jnp.sin(phase)], axis=1).reshape(x_boxes, BOX_X, 2 * nw)

    cos, sin = turn(freqs, np.arange(freqs)[:, None] * np.arange(depth)[None, :])
    forth = np.block([[cos, sin], [-sin, cos]])
    uh, ul = halves(forth)
    ih, il = halves(forth.T * factor)
    last = jnp.logical_and(half, slab == slab_count // 2)
    flags = jnp.stack([odd, last]).astype(jnp.int32)[None, :]
    keep = chunks <= 64
    kept = chunks if keep else 1
    lane_tiles = -(-chunks // 128) * 128
    farm = pl.pallas_call(
        functools.partial(farm_kernel, keep, half, pen_count),
        out_shape=jax.ShapeDtypeStruct((total_blocks, stencil), bf16),
        in_specs=[smem] + [vmem] * 7 + [pl.BlockSpec(memory_space=pl.ANY)],
        out_specs=vmem,
        scratch_shapes=[
            pltpu.VMEM((depth, 2 * own, 2 * nw), f32),
            pltpu.VMEM((2 * own, depth, 2 * nw), f32),
            pltpu.VMEM((z_boxes, 8, 2 * nw), f32),
            pltpu.VMEM((UNROLL, LANES, 2 * nw), f32),
            pltpu.VMEM((kept, LANES, 2 * nw), bf16),
            pltpu.VMEM((kept, LANES, 2 * nw), bf16),
            pltpu.VMEM((kept, 8 * own, LANES), f32),
            pltpu.VMEM((own + 1, 2, freqs, nw), f32),
            pltpu.VMEM((chunks, 16, LANES), f32),
            pltpu.VMEM((chunks, LANES), f32),
            pltpu.VMEM((chunks, 16, LANES), bf16),
            pltpu.VMEM((stencil, total_blocks), f32),
            pltpu.VMEM((-(-kept // TILE), SLOTS, total_blocks if keep else 128), bf16),
            pltpu.VMEM((8, total_blocks), f32),
            pltpu.VMEM((total_blocks, stencil), bf16),
            pltpu.VMEM((1, total_blocks), jnp.int32),
            pltpu.VMEM((2, lane_tiles), jnp.int32),
            pltpu.VMEM((1, chunks * CHUNK), jnp.int32),
            pltpu.SMEM((2, lane_tiles), jnp.int32),
            pltpu.SMEM((1, chunks * CHUNK), jnp.int32),
            pltpu.SemaphoreType.DMA((own + 1, 2)),
            pltpu.SemaphoreType.DMA((2,)),
        ],
        compiler_params=pltpu.CompilerParams(vmem_limit_bytes=58 << 20),
        name="farm",
    )
    partial = farm(flags, packets, ty, tx, jnp.asarray(uh), jnp.asarray(ul), jnp.asarray(ih), jnp.asarray(il), kernel_hat)
    shares = lax.all_to_all(partial.reshape(devices, blocks, stencil), AXES, 0, 0, tiled=True)
    samples = jnp.sum(shares.astype(f32), axis=0).astype(bf16)

    far = jnp.einsum("bps,bs->bp", proj_weight, samples, preferred_element_type=f32)
    driven = charge[pair_source]
    terms = jnp.einsum("tpq,tq->tp", near_matrix, driven, preferred_element_type=f32)
    owners = (pair_target[:, None] == jnp.arange(blocks, dtype=jnp.int32)[None, :]).astype(f32)
    near = jnp.einsum("tb,tp->bp", owners, terms, precision=lax.Precision.HIGHEST)
    total = jnp.where(live, far + near, jnp.zeros_like(far))
    return total.astype(bf16)


def solution(mesh):
    placed = (
        P(AXES, None),
        P(AXES),
        P(AXES, None, None),
        P(AXES, None),
        P(AXES),
        P(AXES),
        P(AXES),
        P(AXES, None, None),
        P(None, None, "slab", "pen"),
    )
    return jax.shard_map(shards, mesh=mesh, in_specs=placed, out_specs=P(AXES, None), check_vma=False)
```

```python
import functools
import math

import jax
import jax.numpy as jnp
import ml_dtypes
import numpy as np
from jax import lax
from jax.experimental import pallas as pl
from jax.experimental.pallas import tpu as pltpu
from jax.sharding import PartitionSpec as P

AXES = ("slab", "pen")
CHUNK = 32
BOX_X = 8
LANES = CHUNK * BOX_X
UNROLL = 4
TILE = 8
SLOTS = TILE * CHUNK
f32 = jnp.float32
bf16 = jnp.bfloat16


def halves(table):
    high = table.astype(ml_dtypes.bfloat16)
    low = (table - high.astype(np.float64)).astype(ml_dtypes.bfloat16)
    return high, low


def split(value):
    high = value.astype(bf16)
    return high, (value - high.astype(f32)).astype(bf16)


def dot(a, b):
    return jnp.dot(a, b, preferred_element_type=f32)


def dot_nt(a, b):
    return lax.dot_general(a, b, (((1,), (1,)), ((), ())), preferred_element_type=f32)


def dot_tn(a, b):
    return lax.dot_general(a, b, (((0,), (0,)), ((), ())), preferred_element_type=f32)


def dot3(a_high, a_low, b_high, b_low):
    left = jnp.concatenate([a_high, a_high, a_low], axis=1)
    return dot(left, jnp.concatenate([b_high, b_low, b_high], axis=0))


def stacked(mul, a_high, a_low, b_high, b_low):
    rows = a_high.shape[0]
    both = mul(jnp.concatenate([a_high, a_low], axis=0), b_high)
    return both[:rows] + (both[rows:] + mul(a_high, b_low))


def row_sums(parts):
    order = [parts[n] for n in (0, 4, 2, 6, 1, 5, 3, 7)]
    for step in (4, 2, 1):
        first = iota(order[0].shape, 0) % (2 * step) < step
        merged = []
        for a, b in zip(order[0::2], order[1::2]):
            kept = jnp.where(first, a, b)
            moved = jnp.where(first, b, a)
            merged.append(kept + (pltpu.roll(moved, 4, 0) if step == 4 else swap_rows(moved, step, first)))
        order = merged
    return order[0]


def swap_rows(value, step, first):
    return jnp.where(first, pltpu.roll(value, 8 - step, 0), pltpu.roll(value, step, 0))


def iota(shape, dim):
    return lax.broadcasted_iota(jnp.int32, shape, dim)


def ones_where(mask):
    return jnp.where(mask, 1.0, 0.0).astype(bf16)


def pack_kernel(grid_shape, charge_ref, live_ref, weight_ref, slab_ref, index_ref, out_ref, packet_ref):
    slab_boxes, row_boxes, x_boxes = grid_shape
    blocks, slots = charge_ref.shape
    counts = jnp.where(iota((blocks, blocks), 0) == iota((blocks, blocks), 1), live_ref[...], 0)
    live = iota((blocks, slots), 1) < jnp.sum(counts, axis=1, keepdims=True)
    charge = jnp.where(live, charge_ref[...].astype(f32), 0.0).astype(bf16)
    for b in range(blocks):
        packet_ref[b : b + 1, :] = dot(charge, weight_ref[b])[b : b + 1]
    packet_ref[blocks : blocks + 8, :] = jnp.zeros((8, slots), f32)
    place, x = index_ref[...] // x_boxes, index_ref[...] % x_boxes
    box = (slab_ref[...] * slab_boxes + place // row_boxes, place % row_boxes, x)
    for n in range(3):
        packet_ref[blocks + n : blocks + n + 1, 0:blocks] = box[n].astype(f32)
    packet = packet_ref[...].astype(bf16)

    def copy(d, carry):
        out_ref[d] = packet
        return carry

    lax.fori_loop(0, out_ref.shape[0], copy, 0)


def farm_kernel(
    keep, half, pens, flag_ref, packets_ref, ty_ref, tx_ref, uh_ref, ul_ref, ih_ref, il_ref, kernel_ref,
    out_ref, grid_ref, cols_ref, edge_ref, ex_ref, eh_ref, el_ref, along_ref, kh_ref, sx_ref, yl_ref, got_ref, acc_ref, hot_ref,
    meta_ref, rows_ref, place_ref, boxes_ref, index_ref, cz_ref, xb_ref, kernel_sems, index_sems,
):
    depth, cv, _ = grid_ref.shape
    z_boxes = depth // 4
    nv = cv // 2
    nw = kh_ref.shape[3]
    freqs = kh_ref.shape[2]
    y_boxes = ty_ref.shape[1] // 2
    blocks = rows_ref.shape[0]
    groups = blocks // 128

    copies = []
    for v in range(nv + 1):
        source = 0 if v == nv else 2 * v + flag_ref[0, 0] if half else v
        for part in range(2):
            copies.append(pltpu.make_async_copy(kernel_ref.at[part, :, source, :], kh_ref.at[v, part], kernel_sems.at[v, part]))
    for copy in copies:
        copy.start()

    own = packets_ref.shape[1] - 8

    def unpack(g, carry):
        meta = jnp.zeros((8, 128), f32)
        for n in range(128 // own):
            d = 128 // own * g + n
            rows_ref[pl.ds(pl.multiple_of(own * d, own), own), :] = packets_ref[d, 0:own, :]
            shift = n % pens * (y_boxes // pens)
            shifted = (iota((8, 128), 0) == 1) & (iota((8, 128), 1) < own)
            part = packets_ref[d, own : own + 8, :].astype(f32) + jnp.where(shifted, float(shift), 0.0)
            meta = meta + (pltpu.roll(part, own * n, 1) if n else part)
        meta_ref[:, pl.ds(pl.multiple_of(128 * g, 128), 128)] = meta
        return carry

    lax.fori_loop(0, groups, unpack, 0, unroll=groups <= 8)
    below = ones_where(iota((128, 128), 0) < iota((128, 128), 1))
    base = jnp.zeros((z_boxes, 128), f32)
    marks, before = [], []
    for g in range(groups):
        box_z = meta_ref[0:1, 128 * g : 128 * g + 128]
        mark = jnp.where(iota((z_boxes, 128), 0) == box_z.astype(jnp.int32), 1.0, 0.0)
        marks.append(mark)
        before.append(base + dot(mark.astype(bf16), below))
        base = base + jnp.sum(mark, axis=1, keepdims=True)
    used = (base.astype(jnp.int32) + (CHUNK - 1)) // CHUNK
    lower = ones_where(iota((z_boxes, z_boxes), 1) < iota((z_boxes, z_boxes), 0))
    start = dot(lower, used.astype(f32).astype(bf16))
    for g in range(groups):
        place = jnp.sum(marks[g] * (start * CHUNK + before[g]), axis=0, keepdims=True)
        place_ref[0:1, 128 * g : 128 * g + 128] = place.astype(jnp.int32)
    end = start.astype(jnp.int32) + used
    for t in range(boxes_ref.shape[1] // 128):
        lane = iota((z_boxes, 128), 1) + 128 * t
        passed = jnp.where(end <= lane, 1, 0)
        boxes_ref[0:1, 128 * t : 128 * t + 128] = jnp.sum(passed, axis=0, keepdims=True)
    boxes_ref[1:2, 0:128] = jnp.sum(used, axis=0, keepdims=True)
    copy = pltpu.make_async_copy(boxes_ref, cz_ref, index_sems.at[0])
    copy.start()

    def clear(z, carry):
        grid_ref[z] = jnp.zeros((cv, 2 * nw), f32)
        return carry

    lax.fori_loop(0, depth, clear, 0)
    edge_ref[...] = jnp.zeros_like(edge_ref)
    copy.wait()
    steps = (cz_ref[1, 0] + (UNROLL - 1)) // UNROLL
    tiles = (UNROLL * steps + TILE - 1) // TILE
    row, col = iota((LANES, LANES), 0), iota((LANES, LANES), 1)
    to_lanes = ones_where((row // CHUNK == col % BOX_X) & (row % CHUNK == col // BOX_X))
    from_lanes = ones_where((col // CHUNK == row % BOX_X) & (col % CHUNK == row // BOX_X))
    row, col = iota((128, 128), 0), iota((128, 128), 1)
    points_first = ones_where((row // 16 == col % BOX_X) & (row % 16 == col // BOX_X))

    def sort(t, carry):
        hot = ones_where(iota((SLOTS, blocks), 0) + SLOTS * t == place_ref[0:1, :])
        if keep:
            hot_ref[t] = hot
        ordered = dot(hot, rows_ref[...]).astype(bf16)
        turned = dot_nt(points_first, ordered)
        lines = exchanged([turned[16 * k : 16 * k + 16] for k in range(BOX_X)])
        lines = dot(jnp.concatenate(lines, axis=0).astype(bf16), to_lanes)
        sx_ref[pl.ds(TILE * t, TILE)] = lines.reshape(TILE, 16, LANES)
        meta = dot_nt(meta_ref[...].astype(bf16), hot)
        index_ref[0:1, pl.ds(pl.multiple_of(SLOTS * t, SLOTS), SLOTS)] = meta[2:3].astype(jnp.int32)
        owned = jnp.where(iota((TILE, SLOTS), 1) // CHUNK == iota((TILE, SLOTS), 0), meta[1:2], 0.0)
        owned = owned[:, :128] + owned[:, 128:]
        owned = owned + pltpu.roll(owned, 64, 1)
        owned = owned + pltpu.roll(owned, 32, 1)
        owned = jnp.concatenate([owned, owned], axis=1).astype(bf16)
        yl_ref[pl.ds(pl.multiple_of(TILE * t, TILE), TILE), :] = dot(owned, to_lanes)
        return carry

    lax.fori_loop(0, tiles, sort, 0)
    copy = pltpu.make_async_copy(index_ref, xb_ref, index_sems.at[1])
    copy.start()
    copy.wait()

    def tables(c, n):
        for b in range(CHUNK):
            ex_ref[n, BOX_X * b : BOX_X * b + BOX_X, :] = tx_ref[xb_ref[0, CHUNK * c + b]]
        hot = ones_where(iota((y_boxes, LANES), 0) == yl_ref[pl.ds(c, 1), :].astype(jnp.int32))
        along = dot(ty_ref[...], jnp.concatenate([hot, hot], axis=0))
        return split(ex_ref[n]), along

    def box_of(c):
        return jnp.minimum(cz_ref[0, c], depth // 4 - 1)

    def scatter(step, carry):
        for n in range(UNROLL):
            c = UNROLL * step + n
            (ex_high, ex_low), along = tables(c, n)
            if keep:
                eh_ref[c], el_ref[c], along_ref[c] = ex_high, ex_low, along
            box = sx_ref[c]
            parts, edges = [], []
            for i in range(4):
                line = [box[4 * i + j : 4 * i + j + 1] for j in range(4)]
                part = along[0:cv] * line[0]
                for j in range(1, 4):
                    part = part + along[cv * j : cv * j + cv] * line[j]
                parts.append(part)
                edges.append((line[0] - line[1]) + (line[2] - line[3]))
            edges.append(jnp.zeros((4, LANES), f32))
            high, low = split(jnp.concatenate(parts + edges, axis=0))
            added = dot3(high, low, ex_high, ex_low)
            where = pl.ds(4 * box_of(c), 4)
            grid_ref[where] = grid_ref[where] + added[: 4 * cv].reshape(4, cv, 2 * nw)
            edge_ref[box_of(c)] = edge_ref[box_of(c)] + added[4 * cv :]
        return carry

    lax.fori_loop(0, steps, scatter, 0)

    def to_columns(g, carry):
        rows = pl.ds(pl.multiple_of(8 * g, 8), 8)
        for z in range(depth // 8):
            piece = grid_ref[8 * z : 8 * z + 8, rows, :]
            cols_ref[rows, 8 * z : 8 * z + 8, :] = jnp.swapaxes(piece, 0, 1)
        return carry

    lax.fori_loop(0, cv // 8, to_columns, 0)

    def filtered(real, imag, kernels):
        field = jnp.concatenate([jnp.concatenate(real, axis=1), jnp.concatenate(imag, axis=1)], axis=0)
        high, low = split(field)
        spec = dot3(uh_ref[...], ul_ref[...], high, low)
        k_re = jnp.concatenate([kh_ref[v, 0] for v in kernels], axis=1)
        k_im = jnp.concatenate([kh_ref[v, 1] for v in kernels], axis=1)
        s_re, s_im = spec[:freqs], spec[freqs:]
        prod = jnp.concatenate([k_re * s_re - k_im * s_im, k_re * s_im + k_im * s_re], axis=0)
        high, low = split(prod)
        back = dot3(ih_ref[...], il_ref[...], high, low)
        return back[:depth], back[depth:]

    pairs = min(8, nv // 2)

    def column(step, carry):
        for p in [pairs * step + n for n in range(pairs)]:
            real, imag = [], []
            for v in (2 * p, 2 * p + 1):
                re, im = cols_ref[v], cols_ref[nv + v]
                real.append(re[:, :nw] - im[:, nw:])
                imag.append(re[:, nw:] + im[:, :nw])
            q_re, q_im = filtered(real, imag, (2 * p, 2 * p + 1))
            for n in range(2):
                part = slice(nw * n, nw * n + nw)
                cols_ref[2 * p + n] = jnp.concatenate([q_re[:, part], q_im[:, part]], axis=1)
                cols_ref[nv + 2 * p + n] = jnp.concatenate([q_im[:, part], -q_re[:, part]], axis=1)
        return carry

    for copy in copies:
        copy.wait()
    lax.fori_loop(0, nv // 2 // pairs, column, 0)

    edge = jnp.concatenate([edge_ref[z][0:4] for z in range(depth // 4)], axis=0)
    q_re, q_im = filtered([edge[:, :nw]], [edge[:, nw:]], (nv,))
    edge = jnp.concatenate([q_re, q_im], axis=1) * flag_ref[0, 1].astype(f32)
    for z in range(depth // 4):
        edge_ref[z, 0:4, :] = edge[4 * z : 4 * z + 4]

    def to_planes(g, carry):
        rows = pl.ds(pl.multiple_of(8 * g, 8), 8)
        for z in range(depth // 8):
            piece = cols_ref[rows, 8 * z : 8 * z + 8, :]
            grid_ref[8 * z : 8 * z + 8, rows, :] = jnp.swapaxes(piece, 0, 1)
        return carry

    lax.fori_loop(0, cv // 8, to_planes, 0)

    def gather(step, carry):
        for n in range(UNROLL):
            c = UNROLL * step + n
            if keep:
                ex_high, ex_low, along = eh_ref[c], el_ref[c], along_ref[c]
            else:
                (ex_high, ex_low), along = tables(c, n)
            planes = grid_ref[pl.ds(4 * box_of(c), 4)].reshape(4 * cv, 2 * nw)
            high, low = split(jnp.concatenate([planes, edge_ref[box_of(c)]], axis=0))
            lines = stacked(dot_nt, high, low, ex_high, ex_low)
            got = []
            for i in (0, 2):
                parts = []
                for n in range(8):
                    at, j = i + n // 4, n % 4
                    part = along[cv * j : cv * j + cv] * lines[cv * at : cv * at + cv]
                    parts.append(jnp.sum(part.reshape(cv // 8, 8, LANES), axis=0))
                first = lines[4 * cv + i : 4 * cv + i + 1]
                second = lines[4 * cv + i + 1 : 4 * cv + i + 2]
                edge = jnp.where(iota((8, LANES), 0) < 4, first, second)
                edge = jnp.where(iota((8, LANES), 0) % 2 == 0, edge, -edge)
                got.append(row_sums(parts) + edge)
            got_ref[c] = jnp.concatenate(got, axis=0).astype(bf16)
        return carry

    lax.fori_loop(0, steps, gather, 0)

    acc_ref[...] = jnp.zeros_like(acc_ref)

    def wipe(c, carry):
        got_ref[c] = jnp.zeros((16, LANES), bf16)
        return carry

    lax.fori_loop(UNROLL * steps, TILE * tiles, wipe, 0)

    def unsort(t, carry):
        lines = got_ref[pl.ds(TILE * t, TILE)].reshape(TILE * 16, LANES)
        lines = dot(lines, from_lanes)
        rows = exchanged([lines[16 * q : 16 * q + 16] for q in range(TILE)])
        hot = hot_ref[t] if keep else ones_where(iota((SLOTS, blocks), 0) + SLOTS * t == place_ref[0:1, :])
        acc_ref[...] += dot(jnp.concatenate(rows, axis=0).astype(bf16), hot)
        return carry

    lax.fori_loop(0, tiles, unsort, 0)
    for g in range(groups):
        part = acc_ref[:, 128 * g : 128 * g + 128].astype(bf16)
        out_ref[128 * g : 128 * g + 128, :] = dot_tn(part, points_first).astype(bf16)


def exchanged(lines):
    lane = iota((16, 128), 1) // CHUNK
    results = []
    for q in range(8):
        tiles = []
        for h in range(2):
            tile = None
            for a in range(4):
                piece = lines[4 * h + a][:, 128 * (q // 4) : 128 * (q // 4) + 128]
                shift = CHUNK * (a - q % 4) % 128
                piece = pltpu.roll(piece, shift, 1) if shift else piece
                tile = piece if tile is None else jnp.where(lane == a, piece, tile)
            tiles.append(tile)
        results.append(jnp.concatenate(tiles, axis=1))
    return results


def turn(length, steps):
    angle = 2.0 * math.pi * (steps % length) / length
    return np.cos(angle), np.sin(angle)


def shards(charges, counts, proj_weight, dest_slab, box_index, pair_target, pair_source, near_matrix, kernel_hat):
    blocks, slots = charges.shape
    stencil = proj_weight.shape[2]
    slab_count = lax.axis_size("slab")
    pen_count = lax.axis_size("pen")
    devices = slab_count * pen_count
    freqs, nv, nw = kernel_hat.shape[1:]
    depth = freqs // 2
    width_y = nv * slab_count
    width_x = nw * pen_count
    planes = freqs // slab_count
    rows_pen = width_y // pen_count
    total_blocks = blocks * devices
    z_boxes, y_boxes, x_boxes = depth // 4, width_y // 4, width_x // BOX_X
    chunks = -(-(total_blocks // CHUNK + z_boxes) // TILE) * TILE
    factor = 1.0 / math.sqrt(float(freqs) * width_y * width_x * total_blocks * stencil)
    slab, pen = lax.axis_index("slab"), lax.axis_index("pen")

    live = jnp.arange(slots, dtype=jnp.int32)[None, :] < counts[:, None]
    charge = jnp.where(live, charges, jnp.zeros_like(charges))
    vmem = pl.BlockSpec(memory_space=pltpu.VMEM)
    smem = pl.BlockSpec(memory_space=pltpu.SMEM)
    pack = pl.pallas_call(
        functools.partial(pack_kernel, (planes // 4, rows_pen // 4, x_boxes)),
        out_shape=jax.ShapeDtypeStruct((devices, blocks + 8, stencil), bf16),
        scratch_shapes=[pltpu.VMEM((blocks + 8, stencil), f32)],
        in_specs=[vmem] * 5,
        out_specs=vmem,
        name="pack",
    )
    packets = pack(charges, counts[None, :], proj_weight, dest_slab.reshape(1, blocks), box_index[None, :])
    packets = lax.all_to_all(packets, AXES, 0, 0, tiled=True)

    v_all, yb_all = np.arange(width_y), np.arange(y_boxes)
    cos, sin = turn(width_y, v_all[None, :, None] * (4 * yb_all[None, None, :] + np.arange(4)[:, None, None]))
    half = nv % 8 == 0
    scale = np.where((v_all == 0) | (not half), 1.0, math.sqrt(2.0))[None, :, None]
    high, low = halves(np.stack([cos * scale, -sin * scale], axis=1))
    along = np.concatenate([high, low], axis=3)
    odd = slab >= slab_count // 2
    own = nv // 2 if half else nv
    if half:
        along = jnp.where(odd, jnp.asarray(along[:, :, 1::2]), jnp.asarray(along[:, :, 0::2]))
    ty = lax.dynamic_slice_in_dim(jnp.asarray(along), slab * own, own, 2).reshape(8 * own, 2 * y_boxes)

    x_all = jnp.arange(width_x, dtype=jnp.int32)[:, None]
    w_own = pen * nw + jnp.arange(nw, dtype=jnp.int32)[None, :]
    phase = (x_all * w_own % width_x).astype(f32) * (2.0 * math.pi / width_x)
    tx = jnp.concatenate([jnp.cos(phase), -jnp.sin(phase)], axis=1).reshape(x_boxes, BOX_X, 2 * nw)

    cos, sin = turn(freqs, np.arange(freqs)[:, None] * np.arange(depth)[None, :])
    forth = np.block([[cos, sin], [-sin, cos]])
    uh, ul = halves(forth)
    ih, il = halves(forth.T * factor)
    last = jnp.logical_and(half, slab == slab_count // 2)
    flags = jnp.stack([odd, last]).astype(jnp.int32)[None, :]
    keep = chunks <= 64
    kept = chunks if keep else 1
    lane_tiles = -(-chunks // 128) * 128
    farm = pl.pallas_call(
        functools.partial(farm_kernel, keep, half, pen_count),
        out_shape=jax.ShapeDtypeStruct((total_blocks, stencil), bf16),
        in_specs=[smem] + [vmem] * 7 + [pl.BlockSpec(memory_space=pl.ANY)],
        out_specs=vmem,
        scratch_shapes=[
            pltpu.VMEM((depth, 2 * own, 2 * nw), f32),
            pltpu.VMEM((2 * own, depth, 2 * nw), f32),
            pltpu.VMEM((z_boxes, 8, 2 * nw), f32),
            pltpu.VMEM((UNROLL, LANES, 2 * nw), f32),
            pltpu.VMEM((kept, LANES, 2 * nw), bf16),
            pltpu.VMEM((kept, LANES, 2 * nw), bf16),
            pltpu.VMEM((kept, 8 * own, LANES), f32),
            pltpu.VMEM((own + 1, 2, freqs, nw), f32),
            pltpu.VMEM((chunks, 16, LANES), f32),
            pltpu.VMEM((chunks, LANES), f32),
            pltpu.VMEM((chunks, 16, LANES), bf16),
            pltpu.VMEM((stencil, total_blocks), f32),
            pltpu.VMEM((-(-kept // TILE), SLOTS, total_blocks if keep else 128), bf16),
            pltpu.VMEM((8, total_blocks), f32),
            pltpu.VMEM((total_blocks, stencil), bf16),
            pltpu.VMEM((1, total_blocks), jnp.int32),
            pltpu.VMEM((2, lane_tiles), jnp.int32),
            pltpu.VMEM((1, chunks * CHUNK), jnp.int32),
            pltpu.SMEM((2, lane_tiles), jnp.int32),
            pltpu.SMEM((1, chunks * CHUNK), jnp.int32),
            pltpu.SemaphoreType.DMA((own + 1, 2)),
            pltpu.SemaphoreType.DMA((2,)),
        ],
        compiler_params=pltpu.CompilerParams(vmem_limit_bytes=58 << 20),
        name="farm",
    )
    partial = farm(flags, packets, ty, tx, jnp.asarray(uh), jnp.asarray(ul), jnp.asarray(ih), jnp.asarray(il), kernel_hat)
    shares = lax.all_to_all(partial.reshape(devices, blocks, stencil), AXES, 0, 0, tiled=True)
    samples = jnp.sum(shares.astype(f32), axis=0).astype(bf16)

    far = jnp.einsum("bps,bs->bp", proj_weight, samples, preferred_element_type=f32)
    driven = charge[pair_source]
    terms = jnp.einsum("tpq,tq->tp", near_matrix, driven, preferred_element_type=f32)
    owners = (pair_target[:, None] == jnp.arange(blocks, dtype=jnp.int32)[None, :]).astype(f32)
    near = jnp.einsum("tb,tp->bp", owners, terms, precision=lax.Precision.HIGHEST)
    total = jnp.where(live, far + near, jnp.zeros_like(far))
    return total.astype(bf16)


def solution(mesh):
    placed = (
        P(AXES, None),
        P(AXES),
        P(AXES, None, None),
        P(AXES, None),
        P(AXES),
        P(AXES),
        P(AXES),
        P(AXES, None, None),
        P(None, None, "slab", "pen"),
    )
    return jax.shard_map(shards, mesh=mesh, in_specs=placed, out_specs=P(AXES, None), check_vma=False)
```
